32 devices in a mesh: dp: 4 (over z), row: 2 (over core), col: 4 (over y, x).
Axes of the slice: x: 2, y: 2, z: 4, core: 2. Of those that a mesh axis runs over, the one named last changes fastest.
Arguments:
- tokens: float32 [1024, 1024], P(('dp', 'row'), 'col'), may hold values from -6 to 6
- segment_ids: int32 [1024], P('dp'), may hold values from 0 to 1023, as said below
- norm_gain: float32 [1024], P('col'), may hold values from 0.5 to 1.5
- in_weight: bfloat16 [1024, 3, 1024], P('col', None, 'row'), may hold values from -0.1875 to 0.1875
- conv_taps: float32 [3, 1024], P(None, ('row', 'col')), may hold values from -3 to 3
- out_weight: bfloat16 [1024, 1024], P('row', 'col'), may hold values from -0.1875 to 0.1875
- ffn_gain: float32 [1024], P('col'), may hold values from 0.5 to 1.5
- gate_weight: bfloat16 [1024, 4608], P('col', 'row'), may hold values from -0.1875 to 0.1875
- up_weight: bfloat16 [1024, 4608], P('col', 'row'), may hold values from -0.1875 to 0.1875
- down_weight: bfloat16 [4608, 1024], P('row', 'col'), may hold values from -0.09375 to 0.09375
- out_grad: float32 [1024, 1024], P(('dp', 'row'), 'col'), may hold values from -6 to 6
Outputs:
- block_out: float32 [1024, 1024], P(('dp', 'row'), 'col')
- in_grad: float32 [1024, 1024], P(('dp', 'row'), 'col')
- grad_norm_gain: float32 [1024], P('col')
- grad_in_weight: float32 [1024, 3, 1024], P('col', None, 'row')
- grad_conv_taps: float32 [3, 1024], P(None, ('row', 'col'))
- grad_out_weight: float32 [1024, 1024], P('row', 'col')
- grad_ffn_gain: float32 [1024], P('col')
- grad_gate_weight: float32 [1024, 4608], P('col', 'row')
- grad_up_weight: float32 [1024, 4608], P('col', 'row')
- grad_down_weight: float32 [4608, 1024], P('row', 'col')
The draws below stay inside these ranges and needn't reach their ends.
Inputs may be any that keep to these rules, and one draw needn't show every extreme that they name: `segment_ids`: ids never fall along the tokens; every aligned sequence of 256 consecutive tokens starts a new id and changes id again at least once inside; runs of one id have 200 to 2000 tokens except where a sequence's start or end cuts them; the last token's id is 1023.
All inputs are finite; a program needn't handle non-finite values.
Results may differ from the reference program's by a relative error of at most 0.0094.
Values may be sent and summed in bfloat16 or wider, within the bound.
No kernel may reach another device: no remote copies, remote signals or barrier semaphores. Data moves between devices by JAX's collectives and lax.ppermute only.
A program may use at most 128 MiB of HBM per device.

```python
import jax
import jax.numpy as jnp
from jax import lax

D = 1024
FF = 4608
DOC_MIN = 200
DOC_MAX = 2000
LEN = 256
TOKENS = 1024


def draw_segment_ids(key, part):
    seq_count = TOKENS // LEN
    doc_slots = LEN // DOC_MIN + 2
    first_key = jax.random.fold_in(key, 11)
    rest_key = jax.random.fold_in(key, 23)
    first_cut = jax.random.randint(first_key, (seq_count, 1), 1, LEN, dtype=jnp.int32)
    rest = jax.random.randint(rest_key, (seq_count, doc_slots), DOC_MIN, DOC_MAX + 1, dtype=jnp.int32)
    lengths = jnp.concatenate([first_cut, rest], axis=1)
    doc_ends = jnp.cumsum(lengths, axis=1)
    positions = jnp.arange(LEN, dtype=jnp.int32)
    within = jnp.sum((doc_ends[:, None, :] <= positions[None, :, None]).astype(jnp.int32), axis=2)
    last_token = jnp.take_along_axis(doc_ends, within, axis=1)
    last_token = jnp.minimum(last_token, LEN) - 1
    ids = last_token + LEN * jnp.arange(seq_count, dtype=jnp.int32)[:, None]
    return ids.reshape(TOKENS).astype(jnp.int32)


def steps_of(key, extent, split, least, high):
    def one(dim, parts):
        draws = jax.random.uniform(jax.random.fold_in(jax.random.fold_in(key, 6), dim), (parts,), jnp.float32, least / len(split), high / len(split))
        return jnp.repeat(jnp.exp(draws), extent[dim] // parts).reshape((-1,) + (1,) * (len(extent) - dim - 1))

    gain = one(*split[0])
    for cut in split[1:]:
        gain = gain * one(*cut)
    return gain


def centred(own_key, shape, deviation, bound, split=(), kind=jnp.bfloat16):
    drawn = deviation * jax.random.normal(own_key, shape, jnp.float32)
    if split:
        drawn = drawn * steps_of(own_key, shape, split, -0.22, 0.18)
    return jnp.clip(drawn, -bound, bound).astype(kind)


def setup_inputs(seed: int = 0) -> dict:
    seeds = jax.random.split(jax.random.key(seed), 12)
    tokens = centred(seeds[0], (TOKENS, D), 1.0, 6.0, ((0, 8), (1, 4)), jnp.float32)
    segment_ids = draw_segment_ids(jax.random.fold_in(seeds[11], 71), 0)
    norm_gain = jnp.clip(1.0 + 0.1 * jax.random.normal(seeds[2], (D,), jnp.float32), 0.5, 1.5)
    in_weight = centred(seeds[3], (D, 3, D), D ** -0.5, 0.1875, ((0, 4), (2, 2)))
    conv_taps = centred(seeds[4], (3, D), 0.6, 3.0, ((1, 8),), jnp.float32)
    out_weight = centred(seeds[5], (D, D), D ** -0.5, 0.1875, ((0, 2), (1, 4)))
    ffn_gain = jnp.clip(1.0 + 0.1 * jax.random.normal(seeds[6], (D,), jnp.float32), 0.5, 1.5)
    gate_weight = centred(seeds[7], (D, FF), D ** -0.5, 0.1875, ((0, 4), (1, 2)))
    up_weight = centred(seeds[8], (D, FF), D ** -0.5, 0.1875, ((0, 4), (1, 2)))
    down_weight = centred(seeds[9], (FF, D), FF ** -0.5, 0.09375, ((0, 2), (1, 4)))
    out_grad = centred(seeds[10], (TOKENS, D), 1.0, 6.0, ((0, 8), (1, 4)), jnp.float32)
    return {"tokens": tokens, "segment_ids": segment_ids, "norm_gain": norm_gain, "in_weight": in_weight, "conv_taps": conv_taps, "out_weight": out_weight, "ffn_gain": ffn_gain, "gate_weight": gate_weight, "up_weight": up_weight, "down_weight": down_weight, "out_grad": out_grad}


epsilon = 1e-05

def shifted(source, amount):
    filler = jnp.zeros((amount,) + source.shape[1:], source.dtype)
    return jnp.concatenate([filler, source[:-amount]], axis=0)

def lifted(source, amount):
    filler = jnp.zeros((amount,) + source.shape[1:], source.dtype)
    return jnp.concatenate([source[amount:], filler], axis=0)

def dot_rows(left, right):
    return lax.dot_general(left, right, (((0,), (0,)), ((), ())), preferred_element_type=jnp.float32)

def dot_cols(left, right):
    return lax.dot_general(left, right, (((1,), (1,)), ((), ())), preferred_element_type=jnp.float32)

def same_masks(segment_ids):
    first = jnp.concatenate([jnp.zeros((1,), jnp.float32), (segment_ids[1:] == segment_ids[:-1]).astype(jnp.float32)])
    second = jnp.concatenate([jnp.zeros((2,), jnp.float32), (segment_ids[2:] == segment_ids[:-2]).astype(jnp.float32)])
    return (first[:, None], second[:, None])

def sequence_pass(tokens, segment_ids, out_grad, params):
    norm_gain, in_weight, conv_taps, out_weight, ffn_gain, gate_weight, up_weight, down_weight = params
    width = tokens.shape[1]
    in_flat = in_weight.reshape(width, 3 * width)
    same_one, same_two = same_masks(segment_ids)
    scale_one = lax.rsqrt(lax.optimization_barrier(jnp.mean(tokens * tokens, axis=1, keepdims=True)) + epsilon)
    normed_one = (tokens * scale_one * norm_gain).astype(jnp.bfloat16)
    mixer_in = jnp.dot(normed_one, in_flat, preferred_element_type=jnp.float32).reshape(-1, 3, width)
    gate_in = mixer_in[:, 0]
    gate_out = mixer_in[:, 1]
    carried = mixer_in[:, 2]
    product = gate_in * carried
    conv_out = conv_taps[2] * product + conv_taps[1] * shifted(product, 1) * same_one + conv_taps[0] * shifted(product, 2) * same_two
    mixed = (gate_out * conv_out).astype(jnp.bfloat16)
    hidden_mid = tokens + jnp.dot(mixed, out_weight, preferred_element_type=jnp.float32)
    scale_two = lax.rsqrt(lax.optimization_barrier(jnp.mean(hidden_mid * hidden_mid, axis=1, keepdims=True)) + epsilon)
    normed_two = (hidden_mid * scale_two * ffn_gain).astype(jnp.bfloat16)
    gate_proj = jnp.dot(normed_two, gate_weight, preferred_element_type=jnp.float32)
    up_proj = jnp.dot(normed_two, up_weight, preferred_element_type=jnp.float32)
    sigmoid_gate = jax.nn.sigmoid(gate_proj)
    activated = (gate_proj * sigmoid_gate * up_proj).astype(jnp.bfloat16)
    block_out = hidden_mid + jnp.dot(activated, down_weight, preferred_element_type=jnp.float32)
    grad_ffn = out_grad.astype(jnp.bfloat16)
    grad_down = dot_rows(activated, grad_ffn)
    grad_act = dot_cols(grad_ffn, down_weight)
    grad_up = (grad_act * gate_proj * sigmoid_gate).astype(jnp.bfloat16)
    grad_gate = (grad_act * up_proj * sigmoid_gate * (1.0 + gate_proj * (1.0 - sigmoid_gate))).astype(jnp.bfloat16)
    grad_gate_w = dot_rows(normed_two, grad_gate)
    grad_up_w = dot_rows(normed_two, grad_up)
    grad_normed_two = dot_cols(grad_gate, gate_weight) + dot_cols(grad_up, up_weight)
    gain_two_grad = lax.optimization_barrier(jnp.sum(grad_normed_two * hidden_mid * scale_two, axis=0))
    weighted_two = ffn_gain * grad_normed_two
    cube_two = scale_two * scale_two * scale_two
    grad_mid = out_grad + scale_two * weighted_two - hidden_mid * cube_two * lax.optimization_barrier(jnp.mean(weighted_two * hidden_mid, axis=1, keepdims=True))
    grad_mix = grad_mid.astype(jnp.bfloat16)
    grad_out_w = dot_rows(mixed, grad_mix)
    grad_mixed = dot_cols(grad_mix, out_weight)
    grad_conv = grad_mixed * gate_out
    grad_product = conv_taps[2] * grad_conv + conv_taps[1] * lifted(grad_conv * same_one, 1) + conv_taps[0] * lifted(grad_conv * same_two, 2)
    taps_grad = jnp.stack([lax.optimization_barrier(jnp.sum(grad_conv * shifted(product, 2) * same_two, axis=0)), lax.optimization_barrier(jnp.sum(grad_conv * shifted(product, 1) * same_one, axis=0)), lax.optimization_barrier(jnp.sum(grad_conv * product, axis=0))])
    grad_triple = jnp.stack([grad_product * carried, grad_mixed * conv_out, grad_product * gate_in], axis=1).astype(jnp.bfloat16)
    flat_grad = grad_triple.reshape(-1, 3 * width)
    grad_in_w = dot_rows(normed_one, flat_grad).reshape(width, 3, width)
    grad_normed_one = dot_cols(flat_grad, in_flat)
    gain_one_grad = lax.optimization_barrier(jnp.sum(grad_normed_one * tokens * scale_one, axis=0))
    weighted_one = norm_gain * grad_normed_one
    cube_one = scale_one * scale_one * scale_one
    in_grad = grad_mid + scale_one * weighted_one - tokens * cube_one * lax.optimization_barrier(jnp.mean(weighted_one * tokens, axis=1, keepdims=True))
    grads = (gain_one_grad, grad_in_w, taps_grad, grad_out_w, gain_two_grad, grad_gate_w, grad_up_w, grad_down)
    return (block_out, in_grad, grads)

def reference(tokens, segment_ids, norm_gain, in_weight, conv_taps, out_weight, ffn_gain, gate_weight, up_weight, down_weight, out_grad):
    seq_count = TOKENS // LEN
    params = (norm_gain, in_weight, conv_taps, out_weight, ffn_gain, gate_weight, up_weight, down_weight)
    stacked = (tokens.reshape(seq_count, LEN, D), segment_ids.reshape(seq_count, LEN), out_grad.reshape(seq_count, LEN, D))
    zeros = (jnp.zeros((D,), jnp.float32), jnp.zeros((D, 3, D), jnp.float32), jnp.zeros((3, D), jnp.float32), jnp.zeros((D, D), jnp.float32), jnp.zeros((D,), jnp.float32), jnp.zeros((D, FF), jnp.float32), jnp.zeros((D, FF), jnp.float32), jnp.zeros((FF, D), jnp.float32))

    def advance(carry, item):
        block_out, in_grad, grads = sequence_pass(item[0], item[1], item[2], params)
        return (jax.tree.map(jnp.add, carry, grads), (block_out, in_grad))
    totals, outputs = lax.scan(advance, zeros, stacked)
    block_out = outputs[0].reshape(TOKENS, D)
    in_grad = outputs[1].reshape(TOKENS, D)
    return (block_out, in_grad, totals[0], totals[1], totals[2], totals[3], totals[4], totals[5], totals[6], totals[7])
```

```python
import jax
import jax.numpy as jnp
from jax import lax
from jax.sharding import PartitionSpec as P

epsilon = 1e-05
f32 = jnp.float32
bf16 = jnp.bfloat16


def dot(left, right, dims):
    return lax.dot_general(left, right, ((dims[:1], dims[1:]), ((), ())), preferred_element_type=f32)


def col_peers():
    n = lax.axis_size("col")
    assert n & (n - 1) == 0
    return range(1, n)


def col_send(piece, k):
    n = lax.axis_size("col")
    return lax.ppermute(piece, "col", [(i, i ^ k) for i in range(n)])


def col_gather(piece):
    return [piece] + [col_send(piece, k) for k in col_peers()]


def row_send(piece):
    n = lax.axis_size("row")
    assert n == 2
    return lax.ppermute(piece, "row", [(i, (i + 1) % n) for i in range(n)])


def in_order(pieces, axis):
    c = lax.axis_index("col")
    n = len(pieces)
    return jnp.concatenate(
        [lax.select_n(c, *[pieces[j ^ cc] for cc in range(n)]) for j in range(n)], axis=axis
    )


def pick(blocks, k):
    c = lax.axis_index("col")
    n = len(blocks)
    return lax.select_n(c, *[blocks[cc ^ k] for cc in range(n)])


def line_sum(part, kind=bf16):
    n = lax.axis_size("dp")
    if n == 1:
        return part.astype(kind).astype(f32)
    if n % 2:
        return lax.psum(part.astype(f32), "dp")
    me = lax.axis_index("dp")
    half = n // 2
    held = part.astype(kind)
    for s in range(half - 1):
        came = lax.ppermute(held, "dp", [(s, s + 1), (n - 1 - s, n - 2 - s)])
        held = (held.astype(f32) + came.astype(f32)).astype(kind)
    came = lax.ppermute(held, "dp", [(half - 1, half), (half, half - 1)])
    held = (held.astype(f32) + came.astype(f32)).astype(kind)
    for s in range(half - 1):
        came = lax.ppermute(
            held, "dp", [(half - 1 - s, half - 2 - s), (half + s, half + 1 + s)]
        )
        got = (me == half - 2 - s) | (me == half + 1 + s)
        held = jnp.where(got, came, held)
    return held.astype(f32)


def scatter_sum(partial, weight):
    half = partial.shape[0] // 2
    mine = partial[:half] + row_send(partial[half:].astype(bf16)).astype(f32)
    rowsum = jnp.sum(mine * weight[:half], axis=1)
    n = lax.axis_size("col")
    width = mine.shape[1] // n
    high = rowsum.astype(bf16)
    low = (rowsum - high.astype(f32)).astype(bf16)
    extra = jnp.zeros((16, width), bf16)
    extra = extra.at[0, :half].set(high).at[1, :half].set(low)
    total = mine[:, :width]
    for k in col_peers():
        sent = jnp.concatenate([mine[:, k * width:(k + 1) * width].astype(bf16), extra], axis=0)
        came = col_send(sent, k).astype(f32)
        total = total + came[:half]
        rowsum = rowsum + came[half, :half] + came[half + 1, :half]
    return total, rowsum[:, None]


def per_device(
    tokens,
    segment_ids,
    norm_gain,
    in_weight,
    conv_taps,
    out_weight,
    ffn_gain,
    gate_weight,
    up_weight,
    down_weight,
    out_grad,
):
    rows, width = tokens.shape
    n_col = lax.axis_size("col")
    n_row = lax.axis_size("row")
    c = lax.axis_index("col")
    r = lax.axis_index("row")
    model = width * n_col
    group = rows * n_row
    lanes = in_weight.shape[2] // n_col
    slice_ff = gate_weight.shape[1] // n_col

    extra = jnp.zeros((8, width), f32).at[0].set(norm_gain).at[1].set(ffn_gain)
    token_parts = col_gather(jnp.concatenate([tokens, extra], axis=0))
    in_blocks = [in_weight[:, :, j * lanes:(j + 1) * lanes].reshape(width, 3 * lanes) for j in range(n_col)]
    in_mine = [pick(in_blocks, 0)] + [col_send(pick(in_blocks, k), k) for k in col_peers()]
    grad_ffn_own = out_grad.astype(bf16)
    shared = col_gather(jnp.concatenate([out_weight, grad_ffn_own], axis=0))
    out_rows = out_weight.shape[0]
    gu_blocks = [
        jnp.concatenate(
            [gate_weight[:, j * slice_ff:(j + 1) * slice_ff], up_weight[:, j * slice_ff:(j + 1) * slice_ff]], axis=1
        )
        for j in range(n_col)
    ]
    gu_mine = [pick(gu_blocks, 0)] + [col_send(pick(gu_blocks, k), k) for k in col_peers()]
    down_rows = [
        lax.dynamic_slice_in_dim(down_weight, (c ^ k) * slice_ff, slice_ff, 0) for k in range(n_col)
    ]
    down_mine = [down_rows[0]] + [col_send(down_rows[k], k) for k in col_peers()]

    gains = jnp.concatenate([p[rows:rows + 2] for p in token_parts], axis=1)
    norm_all, ffn_all = gains[0:1], gains[1:2]
    tok_half = jnp.concatenate([p[:rows] for p in token_parts], axis=1)
    tok = jnp.concatenate([tok_half, row_send(tok_half)], axis=0)
    place = (jnp.arange(group, dtype=jnp.int32) + r * rows) % group
    twice = jnp.concatenate([segment_ids, segment_ids])
    seg = lax.dynamic_slice_in_dim(twice, r * rows, group, 0)
    same_one = ((seg == jnp.roll(seg, 1)) & (place >= 1)).astype(f32)[:, None]
    same_two = ((seg == jnp.roll(seg, 2)) & (place >= 2)).astype(f32)[:, None]

    scale_one = lax.rsqrt(jnp.sum(tok * tok, axis=1, keepdims=True) / model + epsilon)
    normed_one = (tok * scale_one * norm_all).astype(bf16)
    in_full = jnp.concatenate(in_mine, axis=0)
    mixer_in = dot(normed_one, in_full, (1, 0))
    gate_in = mixer_in[:, :lanes]
    gate_out = mixer_in[:, lanes:2 * lanes]
    carried = mixer_in[:, 2 * lanes:]
    product = gate_in * carried
    back_one = jnp.roll(product, 1, axis=0) * same_one
    back_two = jnp.roll(product, 2, axis=0) * same_two
    conv_out = conv_taps[2] * product + conv_taps[1] * back_one + conv_taps[0] * back_two
    mixed = (gate_out * conv_out).astype(bf16)
    mixed_row = in_order(col_gather(mixed), 1)
    mixed_other = row_send(jnp.concatenate([mixed_row[rows:], mixed_row[:rows]], axis=0))
    mixed_all = jnp.concatenate([mixed_row, mixed_other], axis=1)

    shared_half = jnp.concatenate(shared, axis=1)
    shared_other = row_send(shared_half)
    out_all = jnp.concatenate([shared_half[:out_rows], shared_other[:out_rows]], axis=0)
    grad_ffn = jnp.concatenate([shared_half[out_rows:], shared_other[out_rows:]], axis=0)
    hidden = tok + dot(mixed_all, out_all, (1, 0))
    scale_two = lax.rsqrt(jnp.sum(hidden * hidden, axis=1, keepdims=True) / model + epsilon)
    normed_two = (hidden * scale_two * ffn_all).astype(bf16)
    gu_full = jnp.concatenate(gu_mine, axis=0)
    both = dot(normed_two, gu_full, (1, 0))
    gate_proj = both[:, :slice_ff]
    up_proj = both[:, slice_ff:]
    sigmoid_gate = jax.nn.sigmoid(gate_proj)
    activated = (gate_proj * sigmoid_gate * up_proj).astype(bf16)
    act_parts = col_gather(activated)

    grad_ffn_col = grad_ffn[:, :width]
    down_sums = [line_sum(dot(a, grad_ffn_col, (0, 0))) for a in act_parts]

    down_full = jnp.concatenate(down_mine, axis=1)
    grad_act = dot(grad_ffn, down_full, (1, 1))
    grad_up = (grad_act * gate_proj * sigmoid_gate).astype(bf16)
    grad_gate = (grad_act * up_proj * sigmoid_gate * (1.0 + gate_proj * (1.0 - sigmoid_gate))).astype(bf16)
    grad_pair = jnp.concatenate([grad_gate, grad_up], axis=1)
    partial_two = dot(grad_pair, gu_full, (1, 1))
    pair_parts = col_gather(grad_pair)

    grad_normed_two, mean_two = scatter_sum(partial_two, hidden * ffn_all)
    hid = hidden[:rows, :width]
    s2 = scale_two[:rows]
    gain_two_grad = jnp.sum(grad_normed_two * hid * s2, axis=0)
    grad_mid = out_grad + s2 * (ffn_gain * grad_normed_two) - hid * (s2 * s2 * s2) * (mean_two / model)
    grad_mix_half = jnp.concatenate(col_gather(grad_mid.astype(bf16)), axis=1)
    grad_mix = jnp.concatenate([grad_mix_half, row_send(grad_mix_half)], axis=0)

    out_mine = lax.dynamic_slice_in_dim(out_all, c * lanes, lanes, 0)
    grad_mixed = dot(grad_mix, out_mine, (1, 1))
    grad_conv = grad_mixed * gate_out
    lift_one = jnp.roll(grad_conv * same_one, -1, axis=0)
    lift_two = jnp.roll(grad_conv * same_two, -2, axis=0)
    grad_product = conv_taps[2] * grad_conv + conv_taps[1] * lift_one + conv_taps[0] * lift_two
    taps_grad = jnp.stack(
        [
            jnp.sum(grad_conv * back_two, axis=0),
            jnp.sum(grad_conv * back_one, axis=0),
            jnp.sum(grad_conv * product, axis=0),
        ]
    )
    triple = jnp.concatenate(
        [grad_product * carried, grad_mixed * conv_out, grad_product * gate_in], axis=1
    ).astype(bf16)
    partial_one = dot(triple, in_full, (1, 1))
    triple_parts = col_gather(triple)
    grad_normed_one, mean_one = scatter_sum(partial_one, tok * norm_all)
    s1 = scale_one[:rows]
    gain_one_grad = jnp.sum(grad_normed_one * tokens * s1, axis=0)
    in_grad = grad_mid + s1 * (norm_gain * grad_normed_one) - tokens * (s1 * s1 * s1) * (mean_one / model)

    act_all = in_order(act_parts, 1)
    down_out = dot(act_all, down_weight, (1, 0))
    block_out = hid + down_out[:rows] + row_send(down_out[rows:])

    gate_all = in_order([p[:, :slice_ff] for p in pair_parts], 1)
    up_all = in_order([p[:, slice_ff:] for p in pair_parts], 1)
    normed_two_col = normed_two[:, :width]
    gate_sum = line_sum(dot(normed_two_col, gate_all, (0, 0)))
    up_sum = line_sum(dot(normed_two_col, up_all, (0, 0)))
    down_sum = in_order(down_sums, 0)
    out_sum = line_sum(dot(mixed_row, grad_mix[:, :width], (0, 0)))
    triple_all = jnp.concatenate(
        [in_order([p[:, t * lanes:(t + 1) * lanes] for p in triple_parts], 1) for t in range(3)], axis=1
    )
    in_sum = line_sum(dot(normed_one[:, :width], triple_all, (0, 0))).reshape(in_weight.shape)
    gain_pair = jnp.stack([gain_one_grad, gain_two_grad])
    gain_pair = gain_pair + row_send(gain_pair)
    small = jnp.zeros((8, max(width, lanes)), f32)
    small = small.at[0:2, :width].set(gain_pair).at[2:5, :lanes].set(taps_grad)
    small = line_sum(small, f32)
    return (
        block_out,
        in_grad,
        small[0, :width],
        in_sum,
        small[2:5, :lanes],
        out_sum,
        small[1, :width],
        gate_sum,
        up_sum,
        down_sum,
    )


def solution(mesh):
    in_specs = (
        P(("dp", "row"), "col"),
        P("dp"),
        P("col"),
        P("col", None, "row"),
        P(None, ("row", "col")),
        P("row", "col"),
        P("col"),
        P("col", "row"),
        P("col", "row"),
        P("row", "col"),
        P(("dp", "row"), "col"),
    )
    out_specs = (
        P(("dp", "row"), "col"),
        P(("dp", "row"), "col"),
        P("col"),
        P("col", None, "row"),
        P(None, ("row", "col")),
        P("row", "col"),
        P("col"),
        P("col", "row"),
        P("col", "row"),
        P("row", "col"),
    )
    return jax.shard_map(
        per_device, mesh=mesh, in_specs=in_specs, out_specs=out_specs, check_vma=False
    )
```

```python
import jax
import jax.numpy as jnp
from jax import lax
from jax.experimental import pallas as pl
from jax.experimental.pallas import tpu as pltpu
from jax.sharding import PartitionSpec as P

epsilon = 1e-05
f32 = jnp.float32
bf16 = jnp.bfloat16


SMEM = pl.BlockSpec(memory_space=pltpu.SMEM)
VMEM = pl.BlockSpec(memory_space=pltpu.VMEM)


def dot(left, right, ldim, rdim):
    return lax.dot_general(left, right, (((ldim,), (rdim,)), ((), ())), preferred_element_type=f32)


def call(name, body, info, args, outs, scratch=(), flops=10**8):
    size = sum(a.size * a.dtype.itemsize for a in args)
    return pl.pallas_call(
        body,
        out_shape=[jax.ShapeDtypeStruct(s, t) for s, t in outs],
        in_specs=[SMEM] + [VMEM] * len(args),
        out_specs=[VMEM] * len(outs),
        scratch_shapes=list(scratch),
        name=name,
        compiler_params=pltpu.CompilerParams(vmem_limit_bytes=56 * 1024 * 1024),
        cost_estimate=pl.CostEstimate(flops=flops, bytes_accessed=size, transcendentals=0),
    )(info, *args)


def peers():
    n = lax.axis_size("col")
    assert n & (n - 1) == 0
    return range(1, n)


def col_send(piece, k, name):
    n = lax.axis_size("col")
    with jax.named_scope(f"{name}_c{k}"):
        return lax.ppermute(piece, "col", [(i, i ^ k) for i in range(n)])


def row_send(piece, name):
    n = lax.axis_size("row")
    assert n == 2
    with jax.named_scope(f"{name}_r"):
        return lax.ppermute(piece, "row", [(i, (i + 1) % n) for i in range(n)])


def pair_send(piece, name):
    n = lax.axis_size("dp")
    assert n % 2 == 0
    with jax.named_scope(f"{name}_z"):
        return lax.ppermute(piece, "dp", [(i, i ^ 1) for i in range(n)])


def add_to(held, came, kind, name):
    with jax.named_scope(name):
        return (held.astype(f32) + came.astype(f32)).astype(kind)


def line_sum(part, name):
    n = lax.axis_size("dp")
    me = lax.axis_index("dp")
    half = n // 2
    kind = part.dtype
    held = part
    for s in range(half - 1):
        with jax.named_scope(f"{name}_in{s}"):
            came = lax.ppermute(held, "dp", [(s, s + 1), (n - 1 - s, n - 2 - s)])
        held = add_to(held, came, kind, f"{name}_addin{s}")
    with jax.named_scope(f"{name}_mid"):
        came = lax.ppermute(held, "dp", [(half - 1, half), (half, half - 1)])
    held = add_to(held, came, kind, f"{name}_addmid")
    came = held
    for s in range(half - 1):
        with jax.named_scope(f"{name}_out{s}"):
            came = lax.ppermute(held, "dp", [(half - 1 - s, half - 2 - s), (half + s, half + 1 + s)])
        if s < half - 2:
            got = (me == half - 2 - s) | (me == half + 1 + s)
            held = jnp.where(got, came, held)
    return held, came


def far_end():
    n = lax.axis_size("dp")
    me = lax.axis_index("dp")
    return (((me == 0) | (me == n - 1)) & (n > 2)).astype(jnp.int32)


def masks(seg, r, rows, group):
    wide = jnp.broadcast_to(seg, (group, 128))
    wide = jnp.where(r == 0, wide, pltpu.roll(wide, rows, 0))
    place = lax.broadcasted_iota(jnp.int32, (group, 128), 0) + r * rows
    place = jnp.where(place >= group, place - group, place)
    one = jnp.where((wide == pltpu.roll(wide, 1, 0)) & (place >= 1), 1.0, 0.0)
    two = jnp.where((wide == pltpu.roll(wide, 2, 0)) & (place >= 2), 1.0, 0.0)
    return one, two


def per_device(
    tokens,
    segment_ids,
    norm_gain,
    in_weight,
    conv_taps,
    out_weight,
    ffn_gain,
    gate_weight,
    up_weight,
    down_weight,
    out_grad,
):
    rows, width = tokens.shape
    n_col = lax.axis_size("col")
    n_row = lax.axis_size("row")
    c = lax.axis_index("col")
    r = lax.axis_index("row")
    model = width * n_col
    group = rows * n_row
    span = in_weight.shape[2]
    lanes = span // n_col
    hidden_ff = gate_weight.shape[1]
    ff = hidden_ff // n_col
    K = range(n_col)
    hw = width // 2
    ho = span // 2
    info = jnp.stack([c, r, lax.axis_index("dp") % 2, far_end()]).astype(jnp.int32)
    seg = segment_ids[:, None]
    in_t = jnp.transpose(in_weight, (1, 0, 2))

    def prep_first(inf, tok, ng, fg, w, og, pay, gf, *outs):
        cc = inf[0]
        pay[:rows] = tok[...]
        pay[rows:] = jnp.zeros((8, width), f32)
        pay[rows:rows + 1] = ng[...]
        pay[rows + 1:rows + 2] = fg[...]
        gf[...] = og[...].astype(bf16)
        for k in K:
            at = pl.multiple_of((cc ^ k) * lanes, lanes)
            for t in range(3):
                outs[k][:, t * lanes:(t + 1) * lanes] = w[t, :, pl.ds(at, lanes)]

    first = call(
        "prep_first", prep_first, info,
        [tokens, norm_gain[None], ffn_gain[None], in_t, out_grad],
        [((rows + 8, width), f32), ((rows, width), bf16)] + [((width, 3 * lanes), bf16)] * n_col,
    )
    pay0, gf0 = first[:2]
    pays = [pay0] + [col_send(pay0, k, "tok") for k in peers()]
    w_in = [first[2]] + [col_send(first[2 + k], k, "win") for k in peers()]
    pays_o = [row_send(p, f"tok{k}") for k, p in enumerate(pays)]

    def prep_rest(inf, ow, gw, uw, dw, oh, x0, y0, d0, *outs):
        gt, ut = outs[-2:]
        cc, p = inf[0], inf[2]
        oh[...] = ow[pl.ds(pl.multiple_of(p * ho, ho), ho), :]
        gt[...] = gw[...].T
        ut[...] = uw[...].T
        for k in K:
            at = pl.ds(pl.multiple_of((cc ^ k) * ff, 32), ff)
            x = jnp.where(p == 0, gt[at, :], ut[at, :])
            if k == 0:
                x0[...] = x
                y0[...] = jnp.where(p == 0, ut[at, :], gt[at, :])
                d0[...] = dw[at, :]
            else:
                outs[k - 1][...] = x
                outs[n_col - 1 + k - 1][...] = dw[at, pl.ds(pl.multiple_of(p * hw, hw), hw)]

    rest = call(
        "prep_rest", prep_rest, info, [out_weight, gate_weight, up_weight, down_weight],
        [((ho, width), bf16)] + [((ff, width), bf16)] * 3
        + [((ff, width), bf16)] * (n_col - 1) + [((ff, hw), bf16)] * (n_col - 1),
        [pltpu.VMEM((hidden_ff, width), bf16)] * 2,
    )
    out_half, x0, y0, d0 = rest[:4]
    send_x, send_d = rest[4:4 + n_col - 1], rest[4 + n_col - 1:]
    out_a = [col_send(out_half, k, "wout") for k in peers()]
    out_b = [pair_send(a, f"wout{k}") for k, a in enumerate(out_a)]
    xs = [x0] + [col_send(send_x[k - 1], k, "wgu") for k in peers()]
    ys = [y0] + [pair_send(x, f"wgu{k}") for k, x in enumerate(xs) if k]
    gfs = [gf0] + [col_send(gf0, k, "gf") for k in peers()]
    da = [col_send(send_d[k - 1], k, "wdn") for k in peers()]
    db = [pair_send(a, f"wdn{k}") for k, a in enumerate(da)]
    outs_r = [out_weight] + out_a + out_b
    outs_o = [row_send(a, f"wout{i}") for i, a in enumerate(outs_r)]
    gfs_o = [row_send(a, f"gf{i}") for i, a in enumerate(gfs)]

    def mixer(inf, sg, taps, *refs):
        own, oth, w = refs[:n_col], refs[n_col:2 * n_col], refs[2 * n_col:3 * n_col]
        tok, gains, mixed, mix3, n1 = refs[3 * n_col:]
        total = jnp.zeros((group, 1), f32)
        for k in K:
            cols = slice(k * width, (k + 1) * width)
            tok[:rows, cols] = own[k][:rows]
            tok[rows:, cols] = oth[k][:rows]
            gains[:, cols] = own[k][rows:]
            part = tok[:, cols]
            total = total + jnp.sum(part * part, axis=1, keepdims=True)
        scale = lax.rsqrt(total / model + epsilon)
        acc = jnp.zeros((group, 3 * lanes), f32)
        for k in K:
            cols = slice(k * width, (k + 1) * width)
            normed = (tok[:, cols] * scale * gains[0:1, cols]).astype(bf16)
            if k == 0:
                n1[...] = normed
            acc = acc + dot(normed, w[k][...], 1, 0)
        mix3[...] = acc
        one, two = masks(sg[...], inf[1], rows, group)
        product = acc[:, :lanes] * acc[:, 2 * lanes:]
        conv = (
            taps[2:3] * product
            + taps[1:2] * (pltpu.roll(product, 1, 0) * one)
            + taps[0:1] * (pltpu.roll(product, 2, 0) * two)
        )
        mixed[...] = (acc[:, lanes:2 * lanes] * conv).astype(bf16)

    tok, gains, mixed, mix3, n1 = call(
        "mixer", mixer, info, [seg, conv_taps] + pays + pays_o + w_in,
        [
            ((group, model), f32), ((8, model), f32), ((group, lanes), bf16),
            ((group, 3 * lanes), f32), ((group, width), bf16),
        ],
    )
    mixeds = [mixed] + [col_send(mixed, k, "mix") for k in peers()]
    mixeds_o = [row_send(m, f"mix{k}") for k, m in enumerate(mixeds)]

    n_out = 2 * n_col - 1

    def ffn_in(inf, tk, gn, *refs):
        mo, mx = refs[:n_col], refs[n_col:2 * n_col]
        wr = refs[2 * n_col:2 * n_col + n_out]
        wo = refs[2 * n_col + n_out:2 * n_col + 2 * n_out]
        x, y = refs[2 * n_col + 2 * n_out:][:n_col], refs[3 * n_col + 2 * n_out:][:n_col]
        hidden, gp_out, up_out, act_out, n2, ms, mt = refs[4 * n_col + 2 * n_out:]
        cc, p = inf[0], inf[2]
        for k in K:
            at = pl.ds(pl.multiple_of((cc ^ k) * lanes, lanes), lanes)
            ms[:, at] = mo[k][...]
            mt[:rows, at] = mx[k][rows:]
            mt[rows:, at] = mx[k][:rows]
        near = pl.ds(pl.multiple_of(p * ho, ho), ho)
        away = pl.ds(pl.multiple_of((1 - p) * ho, ho), ho)
        total = jnp.zeros((group, 1), f32)
        for k in K:
            cols = slice(k * width, (k + 1) * width)
            h = tk[:, cols]
            for m, w in ((ms, wr), (mt, wo)):
                if k == 0:
                    h = h + dot(m[...], w[0][...], 1, 0)
                else:
                    h = h + dot(m[:, near], w[k][...], 1, 0) + dot(m[:, away], w[n_col - 1 + k][...], 1, 0)
            hidden[:, cols] = h
            total = total + jnp.sum(h * h, axis=1, keepdims=True)
        scale = lax.rsqrt(total / model + epsilon)
        ax = jnp.zeros((ff, group), f32)
        ay = jnp.zeros((ff, group), f32)
        for k in K:
            cols = slice(k * width, (k + 1) * width)
            normed = (hidden[:, cols] * scale * gn[1:2, cols]).astype(bf16)
            if k == 0:
                n2[...] = normed
            ax = ax + dot(x[k][...], normed, 1, 1)
            ay = ay + dot(y[k][...], normed, 1, 1)
        gp = jnp.where(p == 0, ax, ay)
        up = jnp.where(p == 0, ay, ax)
        gp_out[...] = gp
        up_out[...] = up
        act_out[...] = (gp * jax.nn.sigmoid(gp) * up).astype(bf16)

    hidden, gate_proj, up_proj, act, n2 = call(
        "ffn_in", ffn_in, info, [tok, gains] + mixeds + mixeds_o + outs_r + outs_o + xs + ys,
        [
            ((group, model), f32), ((ff, group), f32), ((ff, group), f32), ((ff, group), bf16),
            ((group, width), bf16),
        ],
        [pltpu.VMEM((group, span), bf16)] * 2,
        flops=2 * 10**9,
    )

    def ffn_back(inf, gpr, upr, act_ref, n2r, *refs):
        go, gx = refs[:n_col], refs[n_col:2 * n_col]
        d0r = refs[2 * n_col]
        near, away = refs[2 * n_col + 1:][:n_col - 1], refs[3 * n_col:][:n_col - 1]
        x, y = refs[4 * n_col - 1:][:n_col], refs[5 * n_col - 1:][:n_col]
        piece, chunk, mine, sent, gf = refs[6 * n_col - 1:]
        p = inf[2]
        pn = pl.ds(pl.multiple_of(p * hw, hw), hw)
        pa = pl.ds(pl.multiple_of((1 - p) * hw, hw), hw)
        ga = jnp.zeros((ff, group), f32)
        for k in K:
            gf[k, :rows] = go[k][...]
            gf[k, rows:] = gx[k][...]
            if k == 0:
                ga = ga + dot(d0r[...], gf[0], 1, 1)
            else:
                ga = ga + dot(near[k - 1][...], gf[k, :, pn], 1, 1) + dot(away[k - 1][...], gf[k, :, pa], 1, 1)
        gp, up = gpr[...], upr[...]
        sig = jax.nn.sigmoid(gp)
        gu = (ga * gp * sig).astype(bf16)
        gg = (ga * up * sig * (1.0 + gp * (1.0 - sig))).astype(bf16)
        piece[:ff] = act_ref[...]
        piece[ff:2 * ff] = gg
        piece[2 * ff:] = gu
        chunk[:ff] = dot(act_ref[...], gf[0], 1, 0).astype(bf16)
        chunk[ff:] = dot(piece[ff:], n2r[...], 1, 0).astype(bf16)
        a = jnp.where(p == 0, gg, gu).T
        b = jnp.where(p == 0, gu, gg).T
        for k in K:
            cols = slice(k * width, (k + 1) * width)
            part = dot(a, x[k][...], 1, 0) + dot(b, y[k][...], 1, 0)
            mine[:, cols] = part[:rows]
            sent[:, cols] = part[rows:].astype(bf16)

    piece0, chunk0, mine2, sent2 = call(
        "ffn_back", ffn_back, info,
        [gate_proj, up_proj, act, n2] + gfs + gfs_o + [d0] + da + db + xs + ys,
        [
            ((3 * ff, group), bf16), ((3 * ff, width), bf16), ((rows, model), f32), ((rows, model), bf16),
        ],
        [pltpu.VMEM((n_col, group, width), bf16)],
        flops=2 * 10**9,
    )

    def fold(which):
        def body(inf, mn, came, act_in, gn, own, rs, *outs):
            total = mn[...] + came[...].astype(f32)
            rowsum = jnp.sum(total * act_in[:rows] * gn[which:which + 1], axis=1, keepdims=True)
            line = jnp.broadcast_to(rowsum, (rows, rows)).T[:16]
            high = line.astype(bf16)
            low = (line - high.astype(f32)).astype(bf16)
            own[...] = total[:, :width]
            rs[...] = jnp.broadcast_to(rowsum, (rows, 128))
            for k in peers():
                outs[k - 1][:rows] = total[:, k * width:(k + 1) * width].astype(bf16)
                outs[k - 1][rows:] = jnp.zeros((16, width), bf16)
                outs[k - 1][rows:, :rows] = high
                outs[k - 1][rows:, width - rows:] = low
        return body

    fold_outs = [((rows, width), f32), ((rows, 128), f32)] + [((rows + 16, width), bf16)] * (n_col - 1)

    def unfold(own, rs, came):
        total, line = own[...], jnp.zeros((16, rows), f32)
        for ref in came:
            total = total + ref[:rows].astype(f32)
            line = line + ref[rows:, :rows].astype(f32) + ref[rows:, width - rows:].astype(f32)
        return total, rs[:, :1] + jnp.broadcast_to(line[:1], (rows, rows)).T[:, :1]

    came2 = row_send(sent2, "fold2")
    own2, rs2, *send2 = call("fold2", fold(1), info, [mine2, came2, hidden, gains], fold_outs)
    got2 = [col_send(s, k + 1, "fold2") for k, s in enumerate(send2)]

    def mid(inf, own, rs, hid_ref, gn, og, *refs):
        came, (grad_mid, mix, gain) = refs[:n_col - 1], refs[n_col - 1:]
        total, mean = unfold(own, rs, came)
        full = hid_ref[:rows]
        scale = lax.rsqrt(jnp.sum(full * full, axis=1, keepdims=True) / model + epsilon)
        hid = hid_ref[:rows, :width]
        gm = og[...] + scale * (gn[1:2, :width] * total) - hid * (scale * scale * scale) * (mean / model)
        grad_mid[...] = gm
        mix[...] = gm.astype(bf16)
        gain[...] = jnp.broadcast_to(jnp.sum(total * hid * scale, axis=0, keepdims=True), (8, width))

    grad_mid, gmix0, gain_two = call(
        "mid", mid, info, [own2, rs2, hidden, gains, out_grad] + got2,
        [((rows, width), f32), ((rows, width), bf16), ((8, width), f32)],
    )
    gmix = [gmix0] + [col_send(gmix0, k, "gmix") for k in peers()]
    gmix_o = [row_send(m, f"gmix{k}") for k, m in enumerate(gmix)]

    pieces = [piece0] + [col_send(piece0, k, "piece") for k in peers()]

    def ffn_grad(inf, pc, gfa, gfb, n2r, out, gf):
        gf[:rows] = gfa[...]
        gf[rows:] = gfb[...]
        out[:ff] = dot(pc[:ff], gf[...], 1, 0).astype(bf16)
        out[ff:] = dot(pc[ff:], n2r[...], 1, 0).astype(bf16)

    sums = [line_sum(chunk0, "zf0")]
    for k in peers():
        chunk, = call(
            f"ffn_grad{k}", ffn_grad, info, [pieces[k], gfs[0], gfs_o[0], n2],
            [((3 * ff, width), bf16)], [pltpu.VMEM((group, width), bf16)],
        )
        sums.append(line_sum(chunk, f"zf{k}"))

    def mixer_back(inf, sg, taps, m3, *refs):
        go, gx = refs[:n_col], refs[n_col:2 * n_col]
        w = refs[2 * n_col:2 * n_col + n_out]
        wi = refs[2 * n_col + n_out:][:n_col]
        trip_t, mine, sent, tg = refs[3 * n_col + n_out:]
        cc, p = inf[0], inf[2]
        inside = lax.rem(cc * lanes, ho)
        at = pl.ds(pl.multiple_of(inside, lanes), lanes)
        here = (cc * lanes >= ho) == (p == 1)
        gm = jnp.zeros((group, lanes), f32)
        for k in K:
            if k == 0:
                wk = w[0][pl.ds(pl.multiple_of(cc * lanes, lanes), lanes), :]
            else:
                wk = jnp.where(here, w[k][at, :], w[n_col - 1 + k][at, :])
            gm = gm + dot(jnp.concatenate([go[k][...], gx[k][...]], axis=0), wk, 1, 1)
        one, two = masks(sg[...], inf[1], rows, group)
        gate_in, gate_out, carried = m3[:, :lanes], m3[:, lanes:2 * lanes], m3[:, 2 * lanes:]
        product = gate_in * carried
        back_one = pltpu.roll(product, 1, 0) * one
        back_two = pltpu.roll(product, 2, 0) * two
        conv = taps[2:3] * product + taps[1:2] * back_one + taps[0:1] * back_two
        gc = gm * gate_out
        gpr = (
            taps[2:3] * gc
            + taps[1:2] * pltpu.roll(gc * one, group - 1, 0)
            + taps[0:1] * pltpu.roll(gc * two, group - 2, 0)
        )
        tg[...] = jnp.zeros((8, lanes), f32)
        tg[0:1] = jnp.sum(gc * back_two, axis=0, keepdims=True)
        tg[1:2] = jnp.sum(gc * back_one, axis=0, keepdims=True)
        tg[2:3] = jnp.sum(gc * product, axis=0, keepdims=True)
        triple = jnp.concatenate([gpr * carried, gm * conv, gpr * gate_in], axis=1)
        trip_t[...] = triple.T.astype(bf16)
        low = triple.astype(bf16)
        for k in K:
            cols = slice(k * width, (k + 1) * width)
            part = dot(low, wi[k][...], 1, 1)
            mine[:, cols] = part[:rows]
            sent[:, cols] = part[rows:].astype(bf16)

    trip0, mine1, sent1, taps_grad = call(
        "mixer_back", mixer_back, info, [seg, conv_taps, mix3] + gmix + gmix_o + outs_r + w_in,
        [((3 * lanes, group), bf16), ((rows, model), f32), ((rows, model), bf16), ((8, lanes), f32)],
    )
    trips = [trip0] + [col_send(trip0, k, "trip") for k in peers()]

    def mix_grad(inf, tr, mx, n1r, ga, gb, out, gm):
        gm[:rows] = ga[...]
        gm[rows:] = gb[...]
        out[:3 * lanes] = dot(tr[...], n1r[...], 1, 0).astype(bf16)
        out[3 * lanes:] = dot(mx[...].T, gm[...], 1, 0).astype(bf16)

    for k in K:
        chunk, = call(
            f"mix_grad{k}", mix_grad, info, [trips[k], mixeds[k], n1, gmix[0], gmix_o[0]],
            [((4 * lanes, width), bf16)], [pltpu.VMEM((group, width), bf16)],
        )
        sums.append(line_sum(chunk, f"zm{k}"))

    came1 = row_send(sent1, "fold1")
    own1, rs1, *send1 = call("fold1", fold(0), info, [mine1, came1, tok, gains], fold_outs)
    got1 = [col_send(s, k + 1, "fold1") for k, s in enumerate(send1)]

    def last(inf, own, rs, tk, gn, gmid, *refs):
        came, (out, gain) = refs[:n_col - 1], refs[n_col - 1:]
        total, mean = unfold(own, rs, came)
        full = tk[:rows]
        scale = lax.rsqrt(jnp.sum(full * full, axis=1, keepdims=True) / model + epsilon)
        part = tk[:rows, :width]
        out[...] = gmid[...] + scale * (gn[0:1, :width] * total) - part * (scale * scale * scale) * (mean / model)
        gain[...] = jnp.broadcast_to(jnp.sum(total * part * scale, axis=0, keepdims=True), (8, width))

    in_grad, gain_one = call(
        "last", last, info, [own1, rs1, tok, gains, grad_mid] + got1,
        [((rows, width), f32), ((8, width), f32)],
    )

    def ffn_out(inf, dw, hid, *refs):
        pcs, (mine, sent) = refs[:n_col], refs[n_col:]
        acc = jnp.zeros((group, width), f32)
        for k in K:
            at = pl.ds(pl.multiple_of((inf[0] ^ k) * ff, 32), ff)
            acc = acc + dot(pcs[k][:ff].T, dw[at, :], 1, 0)
        mine[...] = acc[:rows] + hid[:rows, :width]
        sent[...] = acc[rows:]

    out_mine, out_sent = call(
        "ffn_out", ffn_out, info, [down_weight, hidden] + pieces,
        [((rows, width), f32)] * 2,
    )
    block_out = out_mine + row_send(out_sent, "ffn_out")

    gain_pair = jnp.concatenate([gain_one[:1], gain_two[:1]], axis=0)
    gain_pair = gain_pair + row_send(gain_pair, "gains")
    small = jnp.concatenate(
        [gain_pair, jnp.pad(taps_grad[:3], ((0, 0), (0, width - lanes))), jnp.zeros((3, width), f32)], axis=0
    )
    held, came = line_sum(small, "zs")
    small = jnp.where(info[3] == 1, came, held)

    def ffn_place(inf, *refs):
        held_refs, came_refs = refs[:n_col], refs[n_col:2 * n_col]
        gate, up, down, gt, ut = refs[2 * n_col:]
        far = inf[3] == 1
        for k in K:
            at = pl.ds(pl.multiple_of((inf[0] ^ k) * ff, 32), ff)
            for i, dest in enumerate((down, gt, ut)):
                rr = slice(i * ff, (i + 1) * ff)
                dest[at, :] = jnp.where(far, came_refs[k][rr], held_refs[k][rr]).astype(f32)
        gate[...] = gt[...].T
        up[...] = ut[...].T

    gate_sum, up_sum, down_sum = call(
        "ffn_place", ffn_place, info, [s[0] for s in sums[:n_col]] + [s[1] for s in sums[:n_col]],
        [((width, hidden_ff), f32)] * 2 + [((hidden_ff, width), f32)],
        [pltpu.VMEM((hidden_ff, width), f32)] * 2,
    )

    def mix_place(inf, *refs):
        held_refs, came_refs = refs[:n_col], refs[n_col:2 * n_col]
        win, wout = refs[2 * n_col:]
        far = inf[3] == 1
        for k in K:
            at = pl.ds(pl.multiple_of((inf[0] ^ k) * lanes, lanes), lanes)
            for t in range(4):
                rr = slice(t * lanes, (t + 1) * lanes)
                got = jnp.where(far, came_refs[k][rr], held_refs[k][rr]).astype(f32)
                if t < 3:
                    win[t, :, at] = got.T
                else:
                    wout[at, :] = got

    in_sum, out_sum = call(
        "mix_place", mix_place, info, [s[0] for s in sums[n_col:]] + [s[1] for s in sums[n_col:]],
        [((3, width, span), f32), ((span, width), f32)],
    )
    return (
        block_out,
        in_grad,
        small[0],
        jnp.transpose(in_sum, (1, 0, 2)),
        small[2:5, :lanes],
        out_sum,
        small[1],
        gate_sum,
        up_sum,
        down_sum,
    )


def solution(mesh):
    in_specs = (
        P(("dp", "row"), "col"),
        P("dp"),
        P("col"),
        P("col", None, "row"),
        P(None, ("row", "col")),
        P("row", "col"),
        P("col"),
        P("col", "row"),
        P("col", "row"),
        P("row", "col"),
        P(("dp", "row"), "col"),
    )
    out_specs = (
        P(("dp", "row"), "col"),
        P(("dp", "row"), "col"),
        P("col"),
        P("col", None, "row"),
        P(None, ("row", "col")),
        P("row", "col"),
        P("col"),
        P("col", "row"),
        P("col", "row"),
        P("row", "col"),
    )
    return jax.shard_map(
        per_device, mesh=mesh, in_specs=in_specs, out_specs=out_specs, check_vma=False
    )
```

```python
import jax
import jax.numpy as jnp
from jax import lax
from jax.experimental import pallas as pl
from jax.experimental.pallas import tpu as pltpu
from jax.sharding import PartitionSpec as P


epsilon = 1e-05
f32 = jnp.float32
bf16 = jnp.bfloat16


SMEM = pl.BlockSpec(memory_space=pltpu.SMEM)
VMEM = pl.BlockSpec(memory_space=pltpu.VMEM)


def dot(left, right, ldim, rdim):
    return lax.dot_general(left, right, (((ldim,), (rdim,)), ((), ())), preferred_element_type=f32)


def call(body, info, args, outs, scratch=(), flops=10**8):
    size = sum(a.size * a.dtype.itemsize for a in args)
    return pl.pallas_call(
        body,
        out_shape=[jax.ShapeDtypeStruct(s, t) for s, t in outs],
        in_specs=[SMEM] + [VMEM] * len(args),
        out_specs=[VMEM] * len(outs),
        scratch_shapes=list(scratch),
        compiler_params=pltpu.CompilerParams(vmem_limit_bytes=56 * 1024 * 1024),
        cost_estimate=pl.CostEstimate(flops=flops, bytes_accessed=size, transcendentals=0),
    )(info, *args)


def peers():
    n = lax.axis_size("col")
    assert n & (n - 1) == 0
    return range(1, n)


def col_send(piece, k):
    n = lax.axis_size("col")
    return lax.ppermute(piece, "col", [(i, i ^ k) for i in range(n)])


def row_send(piece):
    n = lax.axis_size("row")
    assert n == 2
    return lax.ppermute(piece, "row", [(i, (i + 1) % n) for i in range(n)])


def pair_send(piece):
    n = lax.axis_size("dp")
    assert n % 2 == 0
    return lax.ppermute(piece, "dp", [(i, i ^ 1) for i in range(n)])


def add_to(held, came, kind):
    return (held.astype(f32) + came.astype(f32)).astype(kind)


def line_sum(part):
    n = lax.axis_size("dp")
    me = lax.axis_index("dp")
    half = n // 2
    kind = part.dtype
    held = part
    for s in range(half - 1):
        came = lax.ppermute(held, "dp", [(s, s + 1), (n - 1 - s, n - 2 - s)])
        held = add_to(held, came, kind)
    came = lax.ppermute(held, "dp", [(half - 1, half), (half, half - 1)])
    held = add_to(held, came, kind)
    came = held
    for s in range(half - 1):
        came = lax.ppermute(held, "dp", [(half - 1 - s, half - 2 - s), (half + s, half + 1 + s)])
        if s < half - 2:
            got = (me == half - 2 - s) | (me == half + 1 + s)
            held = jnp.where(got, came, held)
    return held, came


def far_end():
    n = lax.axis_size("dp")
    me = lax.axis_index("dp")
    return (((me == 0) | (me == n - 1)) & (n > 2)).astype(jnp.int32)


def masks(seg, r, rows, group):
    wide = jnp.broadcast_to(seg, (group, 128))
    wide = jnp.where(r == 0, wide, pltpu.roll(wide, rows, 0))
    place = lax.broadcasted_iota(jnp.int32, (group, 128), 0) + r * rows
    place = jnp.where(place >= group, place - group, place)
    one = jnp.where((wide == pltpu.roll(wide, 1, 0)) & (place >= 1), 1.0, 0.0)
    two = jnp.where((wide == pltpu.roll(wide, 2, 0)) & (place >= 2), 1.0, 0.0)
    return one, two


def per_device(
    tokens,
    segment_ids,
    norm_gain,
    in_weight,
    conv_taps,
    out_weight,
    ffn_gain,
    gate_weight,
    up_weight,
    down_weight,
    out_grad,
):
    rows, width = tokens.shape
    n_col = lax.axis_size("col")
    n_row = lax.axis_size("row")
    c = lax.axis_index("col")
    r = lax.axis_index("row")
    model = width * n_col
    group = rows * n_row
    span = in_weight.shape[2]
    lanes = span // n_col
    hidden_ff = gate_weight.shape[1]
    ff = hidden_ff // n_col
    K = range(n_col)
    hw = width // 2
    ho = span // 2
    info = jnp.stack([c, r, lax.axis_index("dp") % 2, far_end()]).astype(jnp.int32)
    seg = segment_ids[:, None]
    in_t = jnp.transpose(in_weight, (1, 0, 2))

    toks = [tokens] + [col_send(tokens, k) for k in peers()]
    toks_o = [row_send(p) for p in toks]

    def prep_first(inf, ng, fg, w, *outs):
        cc = inf[0]
        parts = []
        for g in (ng[...], fg[...]):
            for _ in range(3):
                piece = g.astype(bf16).astype(f32)
                parts.append(piece)
                g = g - piece
        at = lax.broadcasted_iota(jnp.int32, (16, width), 0)
        lines = jnp.zeros((16, width), f32)
        for i, piece in enumerate(parts):
            lines = jnp.where(at == i, jnp.broadcast_to(piece, (16, width)), lines)
        lines = lines.astype(bf16)
        for k in K:
            at = pl.multiple_of((cc ^ k) * lanes, lanes)
            for t in range(3):
                outs[k][:width, t * lanes:(t + 1) * lanes] = w[t, :, pl.ds(at, lanes)]
            outs[k][width:] = jnp.zeros((16, 3 * lanes), bf16)
            outs[k][width:, :width] = lines

    w_in = call(
        prep_first, info, [norm_gain[None], ffn_gain[None], in_t],
        [((width + 16, 3 * lanes), bf16)] * n_col,
    )
    w_in = [w_in[0]] + [col_send(w_in[k], k) for k in peers()]

    last_k = n_col - 1
    fold_ff = ff // 2

    def prep_rest(inf, ow, gw, uw, dw, og, oh, x0, y0, d0, gf, *outs):
        gt, ut = outs[-2:]
        cc, p = inf[0], inf[2]
        oh[...] = ow[pl.ds(pl.multiple_of(p * ho, ho), ho), :]
        gt[...] = gw[...].T
        ut[...] = uw[...].T
        gf[...] = og[...].astype(bf16)
        for k in K:
            at = pl.ds(pl.multiple_of((cc ^ k) * ff, 32), ff)
            x = jnp.where(p == 0, gt[at, :], ut[at, :])
            if k == 0:
                x0[...] = x
                y0[...] = jnp.where(p == 0, ut[at, :], gt[at, :])
                d0[...] = dw[at, :]
            else:
                outs[k - 1][...] = x
                dn = outs[last_k + k - 1]
                if k < last_k:
                    dn[:ff] = dw[at, :]
                    dn[ff:] = gf[...]
                else:
                    part = dw[at, pl.ds(pl.multiple_of(p * hw, hw), hw)]
                    dn[:fold_ff, :hw] = part[:fold_ff]
                    dn[:fold_ff, hw:] = part[fold_ff:]
                    dn[fold_ff:] = gf[...]

    rest = call(
        prep_rest, info, [out_weight, gate_weight, up_weight, down_weight, out_grad],
        [((ho, width), bf16)] + [((ff, width), bf16)] * 3 + [((rows, width), bf16)]
        + [((ff, width), bf16)] * last_k + [((ff + rows, width), bf16)] * (last_k - 1)
        + [((fold_ff + rows, width), bf16)],
        [pltpu.VMEM((hidden_ff, width), bf16)] * 2,
    )
    out_half, x0, y0, d0, gf0 = rest[:5]
    send_x, send_d = rest[5:5 + last_k], rest[5 + last_k:]
    outs_r = [out_weight] + [col_send(out_weight if k < last_k else out_half, k) for k in peers()]
    outs_r.append(pair_send(outs_r[last_k]))
    xs = [x0] + [col_send(send_x[k - 1], k) for k in peers()]
    ys = [y0] + [pair_send(x) for k, x in enumerate(xs) if k]
    downs = [d0] + [col_send(send_d[k - 1], k) for k in peers()]
    gfs = [gf0] + downs[1:]
    gfs_o = [row_send(a) for a in gfs]
    downs.append(pair_send(downs[last_k]))
    n_out = n_col + 1

    def mixer(inf, sg, taps, *refs):
        own, oth, w = refs[:n_col], refs[n_col:2 * n_col], refs[2 * n_col:3 * n_col]
        tok, gains, mixed, mix3, n1 = refs[3 * n_col:]
        total = jnp.zeros((group, 1), f32)
        for k in K:
            cols = slice(k * width, (k + 1) * width)
            tok[:rows, cols] = own[k][...]
            tok[rows:, cols] = oth[k][...]
            for i in range(2):
                gain = w[k][width:, :width].astype(f32)[3 * i:3 * i + 3]
                gains[i:i + 1, cols] = gain[0:1] + gain[1:2] + gain[2:3]
            part = tok[:, cols]
            total = total + jnp.sum(part * part, axis=1, keepdims=True)
        scale = lax.rsqrt(total / model + epsilon)
        acc = jnp.zeros((group, 3 * lanes), f32)
        for k in K:
            cols = slice(k * width, (k + 1) * width)
            normed = (tok[:, cols] * scale * gains[0:1, cols]).astype(bf16)
            if k == 0:
                n1[...] = normed
            acc = acc + dot(normed, w[k][:width], 1, 0)
        mix3[...] = acc
        one, two = masks(sg[...], inf[1], rows, group)
        product = acc[:, :lanes] * acc[:, 2 * lanes:]
        conv = (
            taps[2:3] * product
            + taps[1:2] * (pltpu.roll(product, 1, 0) * one)
            + taps[0:1] * (pltpu.roll(product, 2, 0) * two)
        )
        mixed[...] = (acc[:, lanes:2 * lanes] * conv).astype(bf16)

    tok, gains, mixed, mix3, n1 = call(
        mixer, info, [seg, conv_taps] + toks + toks_o + w_in,
        [
            ((group, model), f32), ((8, model), f32), ((group, lanes), bf16),
            ((group, 3 * lanes), f32), ((group, width), bf16),
        ],
    )
    mixeds = [mixed] + [col_send(mixed, k) for k in peers()]

    def outproj(inf, *refs):
        mo, wr = refs[:n_col], refs[n_col:n_col + n_out]
        hp, ms = refs[n_col + n_out:]
        cc, p = inf[0], inf[2]
        for k in K:
            ms[:, pl.ds(pl.multiple_of((cc ^ k) * lanes, lanes), lanes)] = mo[k][...]
        near = pl.ds(pl.multiple_of(p * ho, ho), ho)
        away = pl.ds(pl.multiple_of((1 - p) * ho, ho), ho)
        for k in K:
            cols = slice(k * width, (k + 1) * width)
            if k < last_k:
                hp[:, cols] = dot(ms[...], wr[k][...], 1, 0)
            else:
                hp[:, cols] = dot(ms[:, near], wr[k][...], 1, 0) + dot(ms[:, away], wr[k + 1][...], 1, 0)

    hp, = call(
        outproj, info, mixeds + outs_r, [((group, model), f32)],
        [pltpu.VMEM((group, span), bf16)],
    )
    hp_o = row_send(hp)

    def ffn_in(inf, tk, gn, mine, other, *refs):
        x, y = refs[:n_col], refs[n_col:2 * n_col]
        hidden, gp_out, up_out, act_out, n2 = refs[2 * n_col:]
        p = inf[2]
        total = jnp.zeros((group, 1), f32)
        for k in K:
            cols = slice(k * width, (k + 1) * width)
            swapped = jnp.concatenate([other[rows:, cols], other[:rows, cols]], axis=0)
            h = tk[:, cols] + (mine[:, cols] + swapped)
            hidden[:, cols] = h
            total = total + jnp.sum(h * h, axis=1, keepdims=True)
        scale = lax.rsqrt(total / model + epsilon)
        ax = jnp.zeros((ff, group), f32)
        ay = jnp.zeros((ff, group), f32)
        for k in K:
            cols = slice(k * width, (k + 1) * width)
            normed = (hidden[:, cols] * scale * gn[1:2, cols]).astype(bf16)
            if k == 0:
                n2[...] = normed
            ax = ax + dot(x[k][...], normed, 1, 1)
            ay = ay + dot(y[k][...], normed, 1, 1)
        gp = jnp.where(p == 0, ax, ay)
        up = jnp.where(p == 0, ay, ax)
        gp_out[...] = gp
        up_out[...] = up
        act_out[...] = (gp * jax.nn.sigmoid(gp) * up).astype(bf16)

    hidden, gate_proj, up_proj, act, n2 = call(
        ffn_in, info, [tok, gains, hp, hp_o] + xs + ys,
        [
            ((group, model), f32), ((ff, group), f32), ((ff, group), f32), ((ff, group), bf16),
            ((group, width), bf16),
        ],
        flops=2 * 10**9,
    )

    cut = 3 * ff // 2

    cut = 3 * ff // 2

    def ffn_back(inf, gpr, upr, act_ref, n2r, *refs):
        go, gx = refs[:n_col], refs[n_col:2 * n_col]
        dn = refs[2 * n_col:3 * n_col + 1]
        piece, chunk_a, chunk_b, gf, chunk = refs[3 * n_col + 1:]
        p = inf[2]
        ga = jnp.zeros((ff, group), f32)
        for k in K:
            skip = go[k].shape[0] - rows
            gf[k, :rows] = go[k][skip:]
            gf[k, rows:] = gx[k][skip:]
            if k < last_k:
                ga = ga + dot(dn[k][:ff], gf[k], 1, 1)
            else:
                near = gf[k, :, pl.ds(pl.multiple_of(p * hw, hw), hw)]
                away = gf[k, :, pl.ds(pl.multiple_of((1 - p) * hw, hw), hw)]
                for g, d in ((near, dn[k]), (away, dn[k + 1])):
                    top = dot(d[:fold_ff, :hw], g, 1, 1)
                    ga = ga + jnp.concatenate([top, dot(d[:fold_ff, hw:], g, 1, 1)], axis=0)
        gp, up = gpr[...], upr[...]
        sig = jax.nn.sigmoid(gp)
        piece[:ff] = act_ref[...]
        piece[ff:2 * ff] = (ga * up * sig * (1.0 + gp * (1.0 - sig))).astype(bf16)
        piece[2 * ff:] = (ga * gp * sig).astype(bf16)
        chunk[:ff] = dot(act_ref[...], gf[0], 1, 0).astype(bf16)
        chunk[ff:] = dot(piece[ff:], n2r[...], 1, 0).astype(bf16)
        chunk_a[...] = chunk[:cut]
        chunk_b[...] = chunk[cut:]

    piece0, chunk_a, chunk_b = call(
        ffn_back, info, [gate_proj, up_proj, act, n2] + gfs + gfs_o + downs,
        [((3 * ff, group), bf16), ((cut, width), bf16), ((3 * ff - cut, width), bf16)],
        [pltpu.VMEM((n_col, group, width), bf16), pltpu.VMEM((3 * ff, width), bf16)],
        flops=2 * 10**9,
    )

    def ffn_part(inf, pc, *refs):
        x, y = refs[:n_col], refs[n_col:2 * n_col]
        mine, sent = refs[2 * n_col:]
        gg, gu = pc[ff:2 * ff], pc[2 * ff:]
        a = jnp.where(inf[2] == 0, gg, gu).T
        b = jnp.where(inf[2] == 0, gu, gg).T
        for k in K:
            cols = slice(k * width, (k + 1) * width)
            part = dot(a, x[k][...], 1, 0) + dot(b, y[k][...], 1, 0)
            mine[:, cols] = part[:rows]
            sent[:, cols] = part[rows:].astype(bf16)

    mine2, sent2 = call(
        ffn_part, info, [piece0] + xs + ys,
        [((rows, model), f32), ((rows, model), bf16)], flops=10**9,
    )

    def fold(which):
        def body(inf, mn, came, act_in, gn, own, rs, *outs):
            total = mn[...] + came[...].astype(f32)
            rowsum = jnp.sum(total * act_in[:rows] * gn[which:which + 1], axis=1, keepdims=True)
            line = jnp.broadcast_to(rowsum, (rows, rows)).T[:16]
            high = line.astype(bf16)
            low = (line - high.astype(f32)).astype(bf16)
            own[...] = total[:, :width]
            rs[...] = jnp.broadcast_to(rowsum, (rows, 128))
            for k in peers():
                outs[k - 1][:rows] = total[:, k * width:(k + 1) * width].astype(bf16)
                outs[k - 1][rows:] = jnp.zeros((16, width), bf16)
                outs[k - 1][rows:, :rows] = high
                outs[k - 1][rows:, width - rows:] = low

        return body

    fold_outs = [((rows, width), f32), ((rows, 128), f32)] + [((rows + 16, width), bf16)] * (n_col - 1)

    def unfold(own, rs, came):
        total, line = own[...], jnp.zeros((16, rows), f32)
        for ref in came:
            total = total + ref[:rows].astype(f32)
            line = line + ref[rows:, :rows].astype(f32) + ref[rows:, width - rows:].astype(f32)
        return total, rs[:, :1] + jnp.broadcast_to(line[:1], (rows, rows)).T[:, :1]

    came2 = row_send(sent2)
    own2, rs2, *send2 = call(fold(1), info, [mine2, came2, hidden, gains], fold_outs)
    got2 = [col_send(s, k + 1) for k, s in enumerate(send2)]

    def mid(inf, own, rs, hid_ref, gn, og, *refs):
        came, (grad_mid, mix, gain) = refs[:n_col - 1], refs[n_col - 1:]
        total, mean = unfold(own, rs, came)
        full = hid_ref[:rows]
        scale = lax.rsqrt(jnp.sum(full * full, axis=1, keepdims=True) / model + epsilon)
        hid = hid_ref[:rows, :width]
        gm = og[...] + scale * (gn[1:2, :width] * total) - hid * (scale * scale * scale) * (mean / model)
        grad_mid[...] = gm
        mix[...] = gm.astype(bf16)
        gain[...] = jnp.broadcast_to(jnp.sum(total * hid * scale, axis=0, keepdims=True), (8, width))

    grad_mid, gmix0, gain_two = call(
        mid, info, [own2, rs2, hidden, gains, out_grad] + got2,
        [((rows, width), f32), ((rows, width), bf16), ((8, width), f32)],
    )
    gmix = [gmix0] + [col_send(gmix0, k) for k in peers()]
    gmix_o = [row_send(m) for m in gmix]

    pieces = [piece0] + [col_send(piece0, k) for k in peers()]

    def ffn_grad(inf, pc, gfa, gfb, n2r, out_a, out_b, gf, out):
        gf[:rows] = gfa[...]
        gf[rows:] = gfb[...]
        out[:ff] = dot(pc[:ff], gf[...], 1, 0).astype(bf16)
        out[ff:] = dot(pc[ff:], n2r[...], 1, 0).astype(bf16)
        out_a[...] = out[:cut]
        out_b[...] = out[cut:]

    ffn_sums = [[line_sum(chunk_a), line_sum(chunk_b)]]
    for k in peers():
        chunk_a, chunk_b = call(
            ffn_grad, info, [pieces[k], gf0, gfs_o[0], n2],
            [((cut, width), bf16), ((3 * ff - cut, width), bf16)],
            [pltpu.VMEM((group, width), bf16), pltpu.VMEM((3 * ff, width), bf16)],
        )
        ffn_sums.append([line_sum(chunk_a), line_sum(chunk_b)])

    def mixer_back(inf, sg, taps, m3, *refs):
        go, gx = refs[:n_col], refs[n_col:2 * n_col]
        w = refs[2 * n_col:2 * n_col + n_out]
        wi = refs[2 * n_col + n_out:][:n_col]
        trip_t, mine, sent, tg = refs[3 * n_col + n_out:]
        cc, p = inf[0], inf[2]
        inside = lax.rem(cc * lanes, ho)
        at = pl.ds(pl.multiple_of(inside, lanes), lanes)
        here = (cc * lanes >= ho) == (p == 1)
        gm = jnp.zeros((group, lanes), f32)
        for k in K:
            if k < last_k:
                wk = w[k][pl.ds(pl.multiple_of(cc * lanes, lanes), lanes), :]
            else:
                wk = jnp.where(here, w[k][at, :], w[k + 1][at, :])
            gm = gm + dot(jnp.concatenate([go[k][...], gx[k][...]], axis=0), wk, 1, 1)
        one, two = masks(sg[...], inf[1], rows, group)
        gate_in, gate_out, carried = m3[:, :lanes], m3[:, lanes:2 * lanes], m3[:, 2 * lanes:]
        product = gate_in * carried
        back_one = pltpu.roll(product, 1, 0) * one
        back_two = pltpu.roll(product, 2, 0) * two
        conv = taps[2:3] * product + taps[1:2] * back_one + taps[0:1] * back_two
        gc = gm * gate_out
        gpr = (
            taps[2:3] * gc
            + taps[1:2] * pltpu.roll(gc * one, group - 1, 0)
            + taps[0:1] * pltpu.roll(gc * two, group - 2, 0)
        )
        tg[...] = jnp.zeros((8, lanes), f32)
        tg[0:1] = jnp.sum(gc * back_two, axis=0, keepdims=True)
        tg[1:2] = jnp.sum(gc * back_one, axis=0, keepdims=True)
        tg[2:3] = jnp.sum(gc * product, axis=0, keepdims=True)
        triple = jnp.concatenate([gpr * carried, gm * conv, gpr * gate_in], axis=1)
        trip_t[...] = triple.T.astype(bf16)
        low = triple.astype(bf16)
        for k in K:
            cols = slice(k * width, (k + 1) * width)
            part = dot(low, wi[k][:width], 1, 1)
            mine[:, cols] = part[:rows]
            sent[:, cols] = part[rows:].astype(bf16)

    trip0, mine1, sent1, taps_grad = call(
        mixer_back, info, [seg, conv_taps, mix3] + gmix + gmix_o + outs_r + w_in,
        [((3 * lanes, group), bf16), ((rows, model), f32), ((rows, model), bf16), ((8, lanes), f32)],
    )
    trips = [trip0] + [col_send(trip0, k) for k in peers()]

    def mix_grad(inf, tr, mx, n1r, ga, gb, out, gm):
        gm[:rows] = ga[...]
        gm[rows:] = gb[...]
        out[:3 * lanes] = dot(tr[...], n1r[...], 1, 0).astype(bf16)
        out[3 * lanes:] = dot(mx[...].T, gm[...], 1, 0).astype(bf16)

    mix_sums = []
    for k in K:
        chunk, = call(
            mix_grad, info, [trips[k], mixeds[k], n1, gmix[0], gmix_o[0]],
            [((4 * lanes, width), bf16)], [pltpu.VMEM((group, width), bf16)],
        )
        mix_sums.append(line_sum(chunk))

    came1 = row_send(sent1)
    own1, rs1, *send1 = call(fold(0), info, [mine1, came1, tok, gains], fold_outs)
    got1 = [col_send(s, k + 1) for k, s in enumerate(send1)]

    def last(inf, own, rs, tk, gn, gmid, *refs):
        came, (out, gain) = refs[:n_col - 1], refs[n_col - 1:]
        total, mean = unfold(own, rs, came)
        full = tk[:rows]
        scale = lax.rsqrt(jnp.sum(full * full, axis=1, keepdims=True) / model + epsilon)
        part = tk[:rows, :width]
        out[...] = gmid[...] + scale * (gn[0:1, :width] * total) - part * (scale * scale * scale) * (mean / model)
        gain[...] = jnp.broadcast_to(jnp.sum(total * part * scale, axis=0, keepdims=True), (8, width))

    in_grad, gain_one = call(
        last, info, [own1, rs1, tok, gains, grad_mid] + got1,
        [((rows, width), f32), ((8, width), f32)],
    )

    def ffn_out(inf, dw, hid, *refs):
        pcs, (mine, sent) = refs[:n_col], refs[n_col:]
        acc = jnp.zeros((group, width), f32)
        for k in K:
            at = pl.ds(pl.multiple_of((inf[0] ^ k) * ff, 32), ff)
            acc = acc + dot(pcs[k][:ff].T, dw[at, :], 1, 0)
        mine[...] = acc[:rows] + hid[:rows, :width]
        sent[...] = acc[rows:]

    out_mine, out_sent = call(
        ffn_out, info, [down_weight, hidden] + pieces,
        [((rows, width), f32)] * 2,
    )
    block_out = out_mine + row_send(out_sent)

    gain_pair = jnp.concatenate([gain_one[:1], gain_two[:1]], axis=0)
    gain_pair = gain_pair + row_send(gain_pair)
    small = jnp.concatenate(
        [gain_pair, jnp.pad(taps_grad[:3], ((0, 0), (0, width - lanes))), jnp.zeros((3, width), f32)], axis=0
    )
    held, came = line_sum(small)
    small = jnp.where(info[3] == 1, came, held)

    def ffn_place(inf, *refs):
        parts, (gate, up, down, whole, gt, ut) = refs[:4 * n_col], refs[4 * n_col:]
        far = inf[3] == 1
        for k in K:
            ha, ca, hb, cb = parts[4 * k:4 * k + 4]
            whole[:cut] = jnp.where(far, ca[...], ha[...])
            whole[cut:] = jnp.where(far, cb[...], hb[...])
            at = pl.ds(pl.multiple_of((inf[0] ^ k) * ff, 32), ff)
            for i, dest in enumerate((down, gt, ut)):
                dest[at, :] = whole[i * ff:(i + 1) * ff].astype(dest.dtype)
        gate[...] = gt[...].T.astype(f32)
        up[...] = ut[...].T.astype(f32)

    gate_sum, up_sum, down_sum = call(
        ffn_place, info, [x for pair in ffn_sums for s in pair for x in s],
        [((width, hidden_ff), f32)] * 2 + [((hidden_ff, width), f32)],
        [pltpu.VMEM((3 * ff, width), bf16)] + [pltpu.VMEM((hidden_ff, width), bf16)] * 2,
    )

    def mix_place(inf, *refs):
        held_refs, came_refs = refs[:n_col], refs[n_col:2 * n_col]
        win, wout = refs[2 * n_col:]
        far = inf[3] == 1
        for k in K:
            at = pl.ds(pl.multiple_of((inf[0] ^ k) * lanes, lanes), lanes)
            for t in range(4):
                rr = slice(t * lanes, (t + 1) * lanes)
                got = jnp.where(far, came_refs[k][rr], held_refs[k][rr])
                if t < 3:
                    win[t, :, at] = got.T.astype(f32)
                else:
                    wout[at, :] = got.astype(f32)

    in_sum, out_sum = call(
        mix_place, info, [s[0] for s in mix_sums] + [s[1] for s in mix_sums],
        [((3, width, span), f32), ((span, width), f32)],
    )
    return (
        block_out,
        in_grad,
        small[0],
        jnp.transpose(in_sum, (1, 0, 2)),
        small[2:5, :lanes],
        out_sum,
        small[1],
        gate_sum,
        up_sum,
        down_sum,
    )


def solution(mesh):
    token = P(("dp", "row"), "col")
    feature, tap = P("col"), P(None, ("row", "col"))
    split_in, split_up, split_down = P("col", None, "row"), P("col", "row"), P("row", "col")
    weights = (feature, split_in, tap, split_down, feature, split_up, split_up, split_down)
    in_specs = (token, P("dp"), *weights, token)
    out_specs = (token, token, *weights)

    return jax.shard_map(per_device, mesh=mesh, in_specs=in_specs, out_specs=out_specs, check_vma=False)
```

```python
import jax
import jax.numpy as jnp
from jax import lax
from jax.experimental import pallas as pl
from jax.experimental.pallas import tpu as pltpu
from jax.sharding import PartitionSpec as P


epsilon = 1e-05
f32 = jnp.float32
bf16 = jnp.bfloat16


SMEM = pl.BlockSpec(memory_space=pltpu.SMEM)
VMEM = pl.BlockSpec(memory_space=pltpu.VMEM)


def dot(left, right, ldim, rdim):
    return lax.dot_general(left, right, (((ldim,), (rdim,)), ((), ())), preferred_element_type=f32)


def call(body, info, args, outs, scratch=(), flops=10**8):
    size = sum(a.size * a.dtype.itemsize for a in args)
    return pl.pallas_call(
        body,
        out_shape=[jax.ShapeDtypeStruct(s, t) for s, t in outs],
        in_specs=[SMEM] + [VMEM] * len(args),
        out_specs=[VMEM] * len(outs),
        scratch_shapes=list(scratch),
        compiler_params=pltpu.CompilerParams(vmem_limit_bytes=56 * 1024 * 1024),
        cost_estimate=pl.CostEstimate(flops=flops, bytes_accessed=size, transcendentals=0),
    )(info, *args)


def peers():
    n = lax.axis_size("col")
    assert n & (n - 1) == 0
    return range(1, n)


def col_send(piece, k):
    n = lax.axis_size("col")
    return lax.ppermute(piece, "col", [(i, i ^ k) for i in range(n)])


def row_send(piece):
    n = lax.axis_size("row")
    assert n == 2
    return lax.ppermute(piece, "row", [(i, (i + 1) % n) for i in range(n)])


def pair_send(piece):
    n = lax.axis_size("dp")
    assert n % 2 == 0
    return lax.ppermute(piece, "dp", [(i, i ^ 1) for i in range(n)])


def add_to(held, came, kind):
    return (held.astype(f32) + came.astype(f32)).astype(kind)


def line_sum(part):
    n = lax.axis_size("dp")
    me = lax.axis_index("dp")
    half = n // 2
    kind = part.dtype
    held = part
    for s in range(half - 1):
        came = lax.ppermute(held, "dp", [(s, s + 1), (n - 1 - s, n - 2 - s)])
        held = add_to(held, came, kind)
    came = lax.ppermute(held, "dp", [(half - 1, half), (half, half - 1)])
    held = add_to(held, came, kind)
    came = held
    for s in range(half - 1):
        came = lax.ppermute(held, "dp", [(half - 1 - s, half - 2 - s), (half + s, half + 1 + s)])
        if s < half - 2:
            got = (me == half - 2 - s) | (me == half + 1 + s)
            held = jnp.where(got, came, held)
    return held, came


LAG = 3


def dp_sums(chunks):
    n = lax.axis_size("dp")
    if n != 4:
        return [line_sum(g) for g in chunks]
    two = lax.axis_size("row")
    ends = [(i, i ^ 1) for i in range(n)]
    inner = [(a * two + r, b * two + r) for a, b in ((1, 2), (2, 1)) for r in range(two)]
    inner += [(a * two + r, a * two + (r + 1) % two) for a in (0, 3) for r in range(two)]
    far = far_end() == 1
    held, came_mid, totals = [], [], []
    for i in range(len(chunks) + LAG):
        t = None
        if i >= LAG:
            t = add_to(held[i - LAG], came_mid[i - LAG], bf16)
        if i >= len(chunks):
            sent = t
        else:
            g = chunks[i]
            sent = g
            if t is not None:
                size = max(g.shape[0], t.shape[0])
                sent = jnp.where(
                    far,
                    jnp.pad(g, ((0, size - g.shape[0]), (0, 0))),
                    jnp.pad(t, ((0, size - t.shape[0]), (0, 0))),
                )
        came = lax.ppermute(sent, "dp", ends)
        if i < len(chunks):
            h = add_to(g, came[:g.shape[0]], bf16)
            held.append(h)
            came_mid.append(lax.ppermute(h, ("dp", "row"), inner))
        if i >= LAG:
            totals.append((sent, came))
    return totals


def far_end():
    n = lax.axis_size("dp")
    me = lax.axis_index("dp")
    return (((me == 0) | (me == n - 1)) & (n > 2)).astype(jnp.int32)


def masks(seg, r, rows, group):
    wide = jnp.broadcast_to(seg, (group, 128))
    wide = jnp.where(r == 0, wide, pltpu.roll(wide, rows, 0))
    place = lax.broadcasted_iota(jnp.int32, (group, 128), 0) + r * rows
    place = jnp.where(place >= group, place - group, place)
    one = jnp.where((wide == pltpu.roll(wide, 1, 0)) & (place >= 1), 1.0, 0.0)
    two = jnp.where((wide == pltpu.roll(wide, 2, 0)) & (place >= 2), 1.0, 0.0)
    return one, two


def per_device(
    tokens,
    segment_ids,
    norm_gain,
    in_weight,
    conv_taps,
    out_weight,
    ffn_gain,
    gate_weight,
    up_weight,
    down_weight,
    out_grad,
):
    rows, width = tokens.shape
    n_col = lax.axis_size("col")
    n_row = lax.axis_size("row")
    c = lax.axis_index("col")
    r = lax.axis_index("row")
    model = width * n_col
    group = rows * n_row
    span = in_weight.shape[2]
    lanes = span // n_col
    hidden_ff = gate_weight.shape[1]
    ff = hidden_ff // n_col
    K = range(n_col)
    hw = width // 2
    ho = span // 2
    info = jnp.stack([c, r, lax.axis_index("dp") % 2, far_end()]).astype(jnp.int32)
    seg = segment_ids[:, None]
    in_t = jnp.transpose(in_weight, (1, 0, 2))

    toks = [tokens] + [col_send(tokens, k) for k in peers()]
    toks_o = [row_send(p) for p in toks]

    def prep_first(inf, ng, fg, w, *outs):
        cc = inf[0]
        parts = []
        for g in (ng[...], fg[...]):
            for _ in range(3):
                piece = g.astype(bf16).astype(f32)
                parts.append(piece)
                g = g - piece
        at = lax.broadcasted_iota(jnp.int32, (16, width), 0)
        lines = jnp.zeros((16, width), f32)
        for i, piece in enumerate(parts):
            lines = jnp.where(at == i, jnp.broadcast_to(piece, (16, width)), lines)
        lines = lines.astype(bf16)
        for k in K:
            at = pl.multiple_of((cc ^ k) * lanes, lanes)
            for t in range(3):
                outs[k][:width, t * lanes:(t + 1) * lanes] = w[t, :, pl.ds(at, lanes)]
            outs[k][width:] = jnp.zeros((16, 3 * lanes), bf16)
            outs[k][width:, :width] = lines

    w_in = call(
        prep_first, info, [norm_gain[None], ffn_gain[None], in_t],
        [((width + 16, 3 * lanes), bf16)] * n_col,
    )
    w_in = [w_in[0]] + [col_send(w_in[k], k) for k in peers()]

    last_k = n_col - 1
    fold_ff = ff // 2

    def prep_rest(inf, ow, gw, uw, dw, og, oh, x0, y0, d0, gf, *outs):
        gt, ut = outs[-2:]
        cc, p = inf[0], inf[2]
        oh[...] = ow[pl.ds(pl.multiple_of(p * ho, ho), ho), :]
        gt[...] = gw[...].T
        ut[...] = uw[...].T
        gf[...] = og[...].astype(bf16)
        for k in K:
            at = pl.ds(pl.multiple_of((cc ^ k) * ff, 32), ff)
            x = jnp.where(p == 0, gt[at, :], ut[at, :])
            if k == 0:
                x0[...] = x
                y0[...] = jnp.where(p == 0, ut[at, :], gt[at, :])
                d0[...] = dw[at, :]
            else:
                outs[k - 1][...] = x
                dn = outs[last_k + k - 1]
                if k < last_k:
                    dn[:ff] = dw[at, :]
                    dn[ff:] = gf[...]
                else:
                    part = dw[at, pl.ds(pl.multiple_of(p * hw, hw), hw)]
                    dn[:fold_ff, :hw] = part[:fold_ff]
                    dn[:fold_ff, hw:] = part[fold_ff:]
                    dn[fold_ff:] = gf[...]

    rest = call(
        prep_rest, info, [out_weight, gate_weight, up_weight, down_weight, out_grad],
        [((ho, width), bf16)] + [((ff, width), bf16)] * 3 + [((rows, width), bf16)]
        + [((ff, width), bf16)] * last_k + [((ff + rows, width), bf16)] * (last_k - 1)
        + [((fold_ff + rows, width), bf16)],
        [pltpu.VMEM((hidden_ff, width), bf16)] * 2,
    )
    out_half, x0, y0, d0, gf0 = rest[:5]
    send_x, send_d = rest[5:5 + last_k], rest[5 + last_k:]
    outs_r = [out_weight] + [col_send(out_weight if k < last_k else out_half, k) for k in peers()]
    outs_r.append(pair_send(outs_r[last_k]))
    xs = [x0] + [col_send(send_x[k - 1], k) for k in peers()]
    ys = [y0] + [pair_send(x) for k, x in enumerate(xs) if k]
    downs = [d0] + [col_send(send_d[k - 1], k) for k in peers()]
    gfs = [gf0] + downs[1:]
    gfs_o = [row_send(a) for a in gfs]
    downs.append(pair_send(downs[last_k]))
    n_out = n_col + 1

    def mixer(inf, sg, taps, *refs):
        own, oth, w = refs[:n_col], refs[n_col:2 * n_col], refs[2 * n_col:3 * n_col]
        tok, gains, mixed, mix3, n1 = refs[3 * n_col:]
        total = jnp.zeros((group, 1), f32)
        for k in K:
            cols = slice(k * width, (k + 1) * width)
            tok[:rows, cols] = own[k][...]
            tok[rows:, cols] = oth[k][...]
            for i in range(2):
                gain = w[k][width:, :width].astype(f32)[3 * i:3 * i + 3]
                gains[i:i + 1, cols] = gain[0:1] + gain[1:2] + gain[2:3]
            part = tok[:, cols]
            total = total + jnp.sum(part * part, axis=1, keepdims=True)
        scale = lax.rsqrt(total / model + epsilon)
        acc = jnp.zeros((group, 3 * lanes), f32)
        for k in K:
            cols = slice(k * width, (k + 1) * width)
            normed = (tok[:, cols] * scale * gains[0:1, cols]).astype(bf16)
            if k == 0:
                n1[...] = normed
            acc = acc + dot(normed, w[k][:width], 1, 0)
        mix3[...] = acc
        one, two = masks(sg[...], inf[1], rows, group)
        product = acc[:, :lanes] * acc[:, 2 * lanes:]
        conv = (
            taps[2:3] * product
            + taps[1:2] * (pltpu.roll(product, 1, 0) * one)
            + taps[0:1] * (pltpu.roll(product, 2, 0) * two)
        )
        mixed[...] = (acc[:, lanes:2 * lanes] * conv).astype(bf16)

    tok, gains, mixed, mix3, n1 = call(
        mixer, info, [seg, conv_taps] + toks + toks_o + w_in,
        [
            ((group, model), f32), ((8, model), f32), ((group, lanes), bf16),
            ((group, 3 * lanes), f32), ((group, width), bf16),
        ],
    )
    mixeds = [mixed] + [col_send(mixed, k) for k in peers()]

    def outproj(inf, *refs):
        mo, wr = refs[:n_col], refs[n_col:n_col + n_out]
        hp, ms = refs[n_col + n_out:]
        cc, p = inf[0], inf[2]
        for k in K:
            ms[:, pl.ds(pl.multiple_of((cc ^ k) * lanes, lanes), lanes)] = mo[k][...]
        near = pl.ds(pl.multiple_of(p * ho, ho), ho)
        away = pl.ds(pl.multiple_of((1 - p) * ho, ho), ho)
        for k in K:
            cols = slice(k * width, (k + 1) * width)
            if k < last_k:
                hp[:, cols] = dot(ms[...], wr[k][...], 1, 0)
            else:
                hp[:, cols] = dot(ms[:, near], wr[k][...], 1, 0) + dot(ms[:, away], wr[k + 1][...], 1, 0)

    hp, = call(
        outproj, info, mixeds + outs_r, [((group, model), f32)],
        [pltpu.VMEM((group, span), bf16)],
    )
    hp_o = row_send(hp)

    def ffn_in(inf, tk, gn, mine, other, *refs):
        x, y = refs[:n_col], refs[n_col:2 * n_col]
        hidden, gp_out, up_out, act_out, n2 = refs[2 * n_col:]
        p = inf[2]
        total = jnp.zeros((group, 1), f32)
        for k in K:
            cols = slice(k * width, (k + 1) * width)
            swapped = jnp.concatenate([other[rows:, cols], other[:rows, cols]], axis=0)
            h = tk[:, cols] + (mine[:, cols] + swapped)
            hidden[:, cols] = h
            total = total + jnp.sum(h * h, axis=1, keepdims=True)
        scale = lax.rsqrt(total / model + epsilon)
        ax = jnp.zeros((ff, group), f32)
        ay = jnp.zeros((ff, group), f32)
        for k in K:
            cols = slice(k * width, (k + 1) * width)
            normed = (hidden[:, cols] * scale * gn[1:2, cols]).astype(bf16)
            if k == 0:
                n2[...] = normed
            ax = ax + dot(x[k][...], normed, 1, 1)
            ay = ay + dot(y[k][...], normed, 1, 1)
        gp = jnp.where(p == 0, ax, ay)
        up = jnp.where(p == 0, ay, ax)
        gp_out[...] = gp
        up_out[...] = up
        act_out[...] = (gp * jax.nn.sigmoid(gp) * up).astype(bf16)

    hidden, gate_proj, up_proj, act, n2 = call(
        ffn_in, info, [tok, gains, hp, hp_o] + xs + ys,
        [
            ((group, model), f32), ((ff, group), f32), ((ff, group), f32), ((ff, group), bf16),
            ((group, width), bf16),
        ],
        flops=2 * 10**9,
    )

    cut = 3 * ff // 2

    cut = 3 * ff // 2

    def ffn_back(inf, gpr, upr, act_ref, n2r, *refs):
        go, gx = refs[:n_col], refs[n_col:2 * n_col]
        dn = refs[2 * n_col:3 * n_col + 1]
        piece, chunk_a, chunk_b, gf, chunk = refs[3 * n_col + 1:]
        p = inf[2]
        ga = jnp.zeros((ff, group), f32)
        for k in K:
            skip = go[k].shape[0] - rows
            gf[k, :rows] = go[k][skip:]
            gf[k, rows:] = gx[k][skip:]
            if k < last_k:
                ga = ga + dot(dn[k][:ff], gf[k], 1, 1)
            else:
                near = gf[k, :, pl.ds(pl.multiple_of(p * hw, hw), hw)]
                away = gf[k, :, pl.ds(pl.multiple_of((1 - p) * hw, hw), hw)]
                for g, d in ((near, dn[k]), (away, dn[k + 1])):
                    top = dot(d[:fold_ff, :hw], g, 1, 1)
                    ga = ga + jnp.concatenate([top, dot(d[:fold_ff, hw:], g, 1, 1)], axis=0)
        gp, up = gpr[...], upr[...]
        sig = jax.nn.sigmoid(gp)
        piece[:ff] = act_ref[...]
        piece[ff:2 * ff] = (ga * up * sig * (1.0 + gp * (1.0 - sig))).astype(bf16)
        piece[2 * ff:] = (ga * gp * sig).astype(bf16)
        chunk[:ff] = dot(act_ref[...], gf[0], 1, 0).astype(bf16)
        chunk[ff:] = dot(piece[ff:], n2r[...], 1, 0).astype(bf16)
        chunk_a[...] = chunk[:cut]
        chunk_b[...] = chunk[cut:]

    piece0, chunk_a, chunk_b = call(
        ffn_back, info, [gate_proj, up_proj, act, n2] + gfs + gfs_o + downs,
        [((3 * ff, group), bf16), ((cut, width), bf16), ((3 * ff - cut, width), bf16)],
        [pltpu.VMEM((n_col, group, width), bf16), pltpu.VMEM((3 * ff, width), bf16)],
        flops=2 * 10**9,
    )

    def ffn_part(inf, pc, *refs):
        x, y = refs[:n_col], refs[n_col:2 * n_col]
        mine, sent = refs[2 * n_col:]
        gg, gu = pc[ff:2 * ff], pc[2 * ff:]
        a = jnp.where(inf[2] == 0, gg, gu).T
        b = jnp.where(inf[2] == 0, gu, gg).T
        for k in K:
            cols = slice(k * width, (k + 1) * width)
            part = dot(a, x[k][...], 1, 0) + dot(b, y[k][...], 1, 0)
            mine[:, cols] = part[:rows]
            sent[:, cols] = part[rows:].astype(bf16)

    mine2, sent2 = call(
        ffn_part, info, [piece0] + xs + ys,
        [((rows, model), f32), ((rows, model), bf16)], flops=10**9,
    )

    def fold(which):
        def body(inf, mn, came, act_in, gn, own, rs, *outs):
            total = mn[...] + came[...].astype(f32)
            rowsum = jnp.sum(total * act_in[:rows] * gn[which:which + 1], axis=1, keepdims=True)
            line = jnp.broadcast_to(rowsum, (rows, rows)).T[:16]
            high = line.astype(bf16)
            low = (line - high.astype(f32)).astype(bf16)
            own[...] = total[:, :width]
            rs[...] = jnp.broadcast_to(rowsum, (rows, 128))
            for k in peers():
                outs[k - 1][:rows] = total[:, k * width:(k + 1) * width].astype(bf16)
                outs[k - 1][rows:] = jnp.zeros((16, width), bf16)
                outs[k - 1][rows:, :rows] = high
                outs[k - 1][rows:, width - rows:] = low

        return body

    fold_outs = [((rows, width), f32), ((rows, 128), f32)] + [((rows + 16, width), bf16)] * (n_col - 1)

    def unfold(own, rs, came):
        total, line = own[...], jnp.zeros((16, rows), f32)
        for ref in came:
            total = total + ref[:rows].astype(f32)
            line = line + ref[rows:, :rows].astype(f32) + ref[rows:, width - rows:].astype(f32)
        return total, rs[:, :1] + jnp.broadcast_to(line[:1], (rows, rows)).T[:, :1]

    came2 = row_send(sent2)
    own2, rs2, *send2 = call(fold(1), info, [mine2, came2, hidden, gains], fold_outs)
    got2 = [col_send(s, k + 1) for k, s in enumerate(send2)]

    def mid(inf, own, rs, hid_ref, gn, og, *refs):
        came, (grad_mid, mix, gain) = refs[:n_col - 1], refs[n_col - 1:]
        total, mean = unfold(own, rs, came)
        full = hid_ref[:rows]
        scale = lax.rsqrt(jnp.sum(full * full, axis=1, keepdims=True) / model + epsilon)
        hid = hid_ref[:rows, :width]
        gm = og[...] + scale * (gn[1:2, :width] * total) - hid * (scale * scale * scale) * (mean / model)
        grad_mid[...] = gm
        mix[...] = gm.astype(bf16)
        gain[...] = jnp.broadcast_to(jnp.sum(total * hid * scale, axis=0, keepdims=True), (8, width))

    grad_mid, gmix0, gain_two = call(
        mid, info, [own2, rs2, hidden, gains, out_grad] + got2,
        [((rows, width), f32), ((rows, width), bf16), ((8, width), f32)],
    )
    gmix = [gmix0] + [col_send(gmix0, k) for k in peers()]
    gmix_o = [row_send(m) for m in gmix]

    pieces = [piece0] + [col_send(piece0, k) for k in peers()]

    def ffn_grad(inf, pc, gfa, gfb, n2r, out_a, out_b, gf, out):
        gf[:rows] = gfa[...]
        gf[rows:] = gfb[...]
        out[:ff] = dot(pc[:ff], gf[...], 1, 0).astype(bf16)
        out[ff:] = dot(pc[ff:], n2r[...], 1, 0).astype(bf16)
        out_a[...] = out[:cut]
        out_b[...] = out[cut:]

    chunks = [chunk_a, chunk_b]
    for k in peers():
        chunk_a, chunk_b = call(
            ffn_grad, info, [pieces[k], gf0, gfs_o[0], n2],
            [((cut, width), bf16), ((3 * ff - cut, width), bf16)],
            [pltpu.VMEM((group, width), bf16), pltpu.VMEM((3 * ff, width), bf16)],
        )
        chunks += [chunk_a, chunk_b]

    def mixer_back(inf, sg, taps, m3, *refs):
        go, gx = refs[:n_col], refs[n_col:2 * n_col]
        w = refs[2 * n_col:2 * n_col + n_out]
        wi = refs[2 * n_col + n_out:][:n_col]
        trip_t, mine, sent, tg = refs[3 * n_col + n_out:]
        cc, p = inf[0], inf[2]
        inside = lax.rem(cc * lanes, ho)
        at = pl.ds(pl.multiple_of(inside, lanes), lanes)
        here = (cc * lanes >= ho) == (p == 1)
        gm = jnp.zeros((group, lanes), f32)
        for k in K:
            if k < last_k:
                wk = w[k][pl.ds(pl.multiple_of(cc * lanes, lanes), lanes), :]
            else:
                wk = jnp.where(here, w[k][at, :], w[k + 1][at, :])
            gm = gm + dot(jnp.concatenate([go[k][...], gx[k][...]], axis=0), wk, 1, 1)
        one, two = masks(sg[...], inf[1], rows, group)
        gate_in, gate_out, carried = m3[:, :lanes], m3[:, lanes:2 * lanes], m3[:, 2 * lanes:]
        product = gate_in * carried
        back_one = pltpu.roll(product, 1, 0) * one
        back_two = pltpu.roll(product, 2, 0) * two
        conv = taps[2:3] * product + taps[1:2] * back_one + taps[0:1] * back_two
        gc = gm * gate_out
        gpr = (
            taps[2:3] * gc
            + taps[1:2] * pltpu.roll(gc * one, group - 1, 0)
            + taps[0:1] * pltpu.roll(gc * two, group - 2, 0)
        )
        tg[...] = jnp.zeros((8, lanes), f32)
        tg[0:1] = jnp.sum(gc * back_two, axis=0, keepdims=True)
        tg[1:2] = jnp.sum(gc * back_one, axis=0, keepdims=True)
        tg[2:3] = jnp.sum(gc * product, axis=0, keepdims=True)
        triple = jnp.concatenate([gpr * carried, gm * conv, gpr * gate_in], axis=1)
        trip_t[...] = triple.T.astype(bf16)
        low = triple.astype(bf16)
        for k in K:
            cols = slice(k * width, (k + 1) * width)
            part = dot(low, wi[k][:width], 1, 1)
            mine[:, cols] = part[:rows]
            sent[:, cols] = part[rows:].astype(bf16)

    trip0, mine1, sent1, taps_grad = call(
        mixer_back, info, [seg, conv_taps, mix3] + gmix + gmix_o + outs_r + w_in,
        [((3 * lanes, group), bf16), ((rows, model), f32), ((rows, model), bf16), ((8, lanes), f32)],
    )
    trips = [trip0] + [col_send(trip0, k) for k in peers()]

    def mix_grad(inf, tr, mx, n1r, ga, gb, out, gm):
        gm[:rows] = ga[...]
        gm[rows:] = gb[...]
        out[:3 * lanes] = dot(tr[...], n1r[...], 1, 0).astype(bf16)
        out[3 * lanes:] = dot(mx[...].T, gm[...], 1, 0).astype(bf16)

    for k in K:
        chunk, = call(
            mix_grad, info, [trips[k], mixeds[k], n1, gmix[0], gmix_o[0]],
            [((4 * lanes, width), bf16)], [pltpu.VMEM((group, width), bf16)],
        )
        chunks.append(chunk)

    came1 = row_send(sent1)
    own1, rs1, *send1 = call(fold(0), info, [mine1, came1, tok, gains], fold_outs)
    got1 = [col_send(s, k + 1) for k, s in enumerate(send1)]

    def last(inf, own, rs, tk, gn, gmid, *refs):
        came, (out, gain) = refs[:n_col - 1], refs[n_col - 1:]
        total, mean = unfold(own, rs, came)
        full = tk[:rows]
        scale = lax.rsqrt(jnp.sum(full * full, axis=1, keepdims=True) / model + epsilon)
        part = tk[:rows, :width]
        out[...] = gmid[...] + scale * (gn[0:1, :width] * total) - part * (scale * scale * scale) * (mean / model)
        gain[...] = jnp.broadcast_to(jnp.sum(total * part * scale, axis=0, keepdims=True), (8, width))

    in_grad, gain_one = call(
        last, info, [own1, rs1, tok, gains, grad_mid] + got1,
        [((rows, width), f32), ((8, width), f32)],
    )

    def ffn_out(inf, dw, hid, *refs):
        pcs, (mine, sent) = refs[:n_col], refs[n_col:]
        acc = jnp.zeros((group, width), f32)
        for k in K:
            at = pl.ds(pl.multiple_of((inf[0] ^ k) * ff, 32), ff)
            acc = acc + dot(pcs[k][:ff].T, dw[at, :], 1, 0)
        mine[...] = acc[:rows] + hid[:rows, :width]
        sent[...] = acc[rows:]

    out_mine, out_sent = call(
        ffn_out, info, [down_weight, hidden] + pieces,
        [((rows, width), f32)] * 2,
    )
    block_out = out_mine + row_send(out_sent)

    gain_pair = jnp.concatenate([gain_one[:1], gain_two[:1]], axis=0)
    gain_pair = gain_pair + row_send(gain_pair)
    taps = jnp.pad(taps_grad[:3], ((0, 0), (0, width - lanes)))
    chunks.append(jnp.pad(jnp.concatenate([gain_pair, taps], axis=0), ((0, 11), (0, 0))).astype(bf16))
    sums = dp_sums(chunks)
    small = jnp.where(info[3] == 1, sums[-1][1], sums[-1][0]).astype(f32)

    def ffn_place(inf, *refs):
        parts, (gate, up, down, whole, gt, ut) = refs[:4 * n_col], refs[4 * n_col:]
        far = inf[3] == 1
        for k in K:
            ha, ca, hb, cb = parts[4 * k:4 * k + 4]
            whole[:cut] = jnp.where(far, ca[:cut], ha[:cut])
            whole[cut:] = jnp.where(far, cb[:cut], hb[:cut])
            at = pl.ds(pl.multiple_of((inf[0] ^ k) * ff, 32), ff)
            for i, dest in enumerate((down, gt, ut)):
                dest[at, :] = whole[i * ff:(i + 1) * ff].astype(dest.dtype)
        gate[...] = gt[...].T.astype(f32)
        up[...] = ut[...].T.astype(f32)

    gate_sum, up_sum, down_sum = call(
        ffn_place, info, [x for s in sums[:2 * n_col] for x in s],
        [((width, hidden_ff), f32)] * 2 + [((hidden_ff, width), f32)],
        [pltpu.VMEM((3 * ff, width), bf16)] + [pltpu.VMEM((hidden_ff, width), bf16)] * 2,
    )

    def mix_place(inf, *refs):
        held_refs, came_refs = refs[:n_col], refs[n_col:2 * n_col]
        win, wout = refs[2 * n_col:]
        far = inf[3] == 1
        for k in K:
            at = pl.ds(pl.multiple_of((inf[0] ^ k) * lanes, lanes), lanes)
            for t in range(4):
                rr = slice(t * lanes, (t + 1) * lanes)
                got = jnp.where(far, came_refs[k][rr], held_refs[k][rr])
                if t < 3:
                    win[t, :, at] = got.T.astype(f32)
                else:
                    wout[at, :] = got.astype(f32)

    in_sum, out_sum = call(
        mix_place, info, [s[0] for s in sums[2 * n_col:-1]] + [s[1] for s in sums[2 * n_col:-1]],
        [((3, width, span), f32), ((span, width), f32)],
    )
    return (
        block_out,
        in_grad,
        small[0],
        jnp.transpose(in_sum, (1, 0, 2)),
        small[2:5, :lanes],
        out_sum,
        small[1],
        gate_sum,
        up_sum,
        down_sum,
    )


def solution(mesh):
    token = P(("dp", "row"), "col")
    feature, tap = P("col"), P(None, ("row", "col"))
    split_in, split_up, split_down = P("col", None, "row"), P("col", "row"), P("row", "col")
    weights = (feature, split_in, tap, split_down, feature, split_up, split_up, split_down)
    in_specs = (token, P("dp"), *weights, token)
    out_specs = (token, token, *weights)

    return jax.shard_map(per_device, mesh=mesh, in_specs=in_specs, out_specs=out_specs, check_vma=False)
```

```python
import jax
import jax.numpy as jnp
from jax import lax
from jax.experimental import pallas as pl
from jax.experimental.pallas import tpu as pltpu
from jax.sharding import PartitionSpec as P


epsilon = 1e-05
f32 = jnp.float32
bf16 = jnp.bfloat16


SMEM = pl.BlockSpec(memory_space=pltpu.SMEM)
VMEM = pl.BlockSpec(memory_space=pltpu.VMEM)


def dot(left, right, ldim, rdim):
    return lax.dot_general(left, right, (((ldim,), (rdim,)), ((), ())), preferred_element_type=f32)


def call(body, info, args, outs, scratch=(), flops=10**8):
    size = sum(a.size * a.dtype.itemsize for a in args)
    return pl.pallas_call(
        body,
        out_shape=[jax.ShapeDtypeStruct(s, t) for s, t in outs],
        in_specs=[SMEM] + [VMEM] * len(args),
        out_specs=[VMEM] * len(outs),
        scratch_shapes=list(scratch),
        compiler_params=pltpu.CompilerParams(vmem_limit_bytes=56 * 1024 * 1024),
        cost_estimate=pl.CostEstimate(flops=flops, bytes_accessed=size, transcendentals=0),
    )(info, *args)


def peers():
    n = lax.axis_size("col")
    assert n & (n - 1) == 0
    return range(1, n)


def col_send(piece, k):
    n = lax.axis_size("col")
    return lax.ppermute(piece, "col", [(i, i ^ k) for i in range(n)])


def row_send(piece):
    n = lax.axis_size("row")
    assert n == 2
    return lax.ppermute(piece, "row", [(i, (i + 1) % n) for i in range(n)])


def pair_send(piece):
    n = lax.axis_size("dp")
    assert n % 2 == 0
    return lax.ppermute(piece, "dp", [(i, i ^ 1) for i in range(n)])


def add_to(held, came, kind):
    return (held.astype(f32) + came.astype(f32)).astype(kind)


def line_sum(part):
    n = lax.axis_size("dp")
    me = lax.axis_index("dp")
    half = n // 2
    kind = part.dtype
    held = part
    for s in range(half - 1):
        came = lax.ppermute(held, "dp", [(s, s + 1), (n - 1 - s, n - 2 - s)])
        held = add_to(held, came, kind)
    came = lax.ppermute(held, "dp", [(half - 1, half), (half, half - 1)])
    held = add_to(held, came, kind)
    came = held
    for s in range(half - 1):
        came = lax.ppermute(held, "dp", [(half - 1 - s, half - 2 - s), (half + s, half + 1 + s)])
        if s < half - 2:
            got = (me == half - 2 - s) | (me == half + 1 + s)
            held = jnp.where(got, came, held)
    return held, came


LAG = 3


def dp_sums(chunks):
    n = lax.axis_size("dp")
    if n != 4:
        return [line_sum(g) for g in chunks]
    two = lax.axis_size("row")
    ends = [(i, i ^ 1) for i in range(n)]
    inner = [(a * two + r, b * two + r) for a, b in ((1, 2), (2, 1)) for r in range(two)]
    inner += [(a * two + r, a * two + (r + 1) % two) for a in (0, 3) for r in range(two)]
    far = far_end() == 1
    held, came_mid, totals = [], [], []
    for i in range(len(chunks) + LAG):
        t = None
        if i >= LAG:
            t = add_to(held[i - LAG], came_mid[i - LAG], bf16)
        if i >= len(chunks):
            sent = t
        else:
            g = chunks[i]
            sent = g
            if t is not None:
                size = max(g.shape[0], t.shape[0])
                sent = jnp.where(
                    far,
                    jnp.pad(g, ((0, size - g.shape[0]), (0, 0))),
                    jnp.pad(t, ((0, size - t.shape[0]), (0, 0))),
                )
        came = lax.ppermute(sent, "dp", ends)
        if i < len(chunks):
            h = add_to(g, came[:g.shape[0]], bf16)
            held.append(h)
            came_mid.append(lax.ppermute(h, ("dp", "row"), inner))
        if i >= LAG:
            totals.append((sent, came))
    return totals


def far_end():
    n = lax.axis_size("dp")
    me = lax.axis_index("dp")
    return (((me == 0) | (me == n - 1)) & (n > 2)).astype(jnp.int32)


def masks(seg, r, rows, group):
    wide = jnp.broadcast_to(seg, (group, 128))
    wide = jnp.where(r == 0, wide, pltpu.roll(wide, rows, 0))
    place = lax.broadcasted_iota(jnp.int32, (group, 128), 0) + r * rows
    place = jnp.where(place >= group, place - group, place)
    one = jnp.where((wide == pltpu.roll(wide, 1, 0)) & (place >= 1), 1.0, 0.0)
    two = jnp.where((wide == pltpu.roll(wide, 2, 0)) & (place >= 2), 1.0, 0.0)
    return one, two


def per_device(
    tokens,
    segment_ids,
    norm_gain,
    in_weight,
    conv_taps,
    out_weight,
    ffn_gain,
    gate_weight,
    up_weight,
    down_weight,
    out_grad,
):
    rows, width = tokens.shape
    n_col = lax.axis_size("col")
    n_row = lax.axis_size("row")
    c = lax.axis_index("col")
    r = lax.axis_index("row")
    model = width * n_col
    group = rows * n_row
    span = in_weight.shape[2]
    lanes = span // n_col
    hidden_ff = gate_weight.shape[1]
    ff = hidden_ff // n_col
    K = range(n_col)
    hw = width // 2
    ho = span // 2
    info = jnp.stack([c, r, lax.axis_index("dp") % 2, far_end()]).astype(jnp.int32)
    seg = segment_ids[:, None]
    in_t = jnp.transpose(in_weight, (1, 0, 2))

    toks = [tokens] + [col_send(tokens, k) for k in peers()]
    toks_o = [row_send(p) for p in toks]

    def prep_first(inf, ng, fg, w, *outs):
        cc = inf[0]
        parts = []
        for g in (ng[...], fg[...]):
            for _ in range(3):
                piece = g.astype(bf16).astype(f32)
                parts.append(piece)
                g = g - piece
        at = lax.broadcasted_iota(jnp.int32, (16, width), 0)
        lines = jnp.zeros((16, width), f32)
        for i, piece in enumerate(parts):
            lines = jnp.where(at == i, jnp.broadcast_to(piece, (16, width)), lines)
        lines = lines.astype(bf16)
        for k in K:
            at = pl.multiple_of((cc ^ k) * lanes, lanes)
            for t in range(3):
                outs[k][:width, t * lanes:(t + 1) * lanes] = w[t, :, pl.ds(at, lanes)]
            outs[k][width:] = jnp.zeros((16, 3 * lanes), bf16)
            outs[k][width:, :width] = lines

    w_in = call(
        prep_first, info, [norm_gain[None], ffn_gain[None], in_t],
        [((width + 16, 3 * lanes), bf16)] * n_col,
    )
    w_in = [w_in[0]] + [col_send(w_in[k], k) for k in peers()]

    last_k = n_col - 1
    fold_ff = ff // 2

    def prep_rest(inf, ow, gw, uw, dw, og, oh, x0, y0, d0, gf, *outs):
        gt, ut = outs[-2:]
        cc, p = inf[0], inf[2]
        oh[...] = ow[pl.ds(pl.multiple_of(p * ho, ho), ho), :]
        gt[...] = gw[...].T
        ut[...] = uw[...].T
        gf[...] = og[...].astype(bf16)
        for k in K:
            at = pl.ds(pl.multiple_of((cc ^ k) * ff, 32), ff)
            x = jnp.where(p == 0, gt[at, :], ut[at, :])
            if k == 0:
                x0[...] = x
                y0[...] = jnp.where(p == 0, ut[at, :], gt[at, :])
                d0[...] = dw[at, :]
            else:
                outs[k - 1][...] = x
                dn = outs[last_k + k - 1]
                if k < last_k:
                    dn[:ff] = dw[at, :]
                    dn[ff:] = gf[...]
                else:
                    part = dw[at, pl.ds(pl.multiple_of(p * hw, hw), hw)]
                    dn[:fold_ff, :hw] = part[:fold_ff]
                    dn[:fold_ff, hw:] = part[fold_ff:]
                    dn[fold_ff:] = gf[...]

    rest = call(
        prep_rest, info, [out_weight, gate_weight, up_weight, down_weight, out_grad],
        [((ho, width), bf16)] + [((ff, width), bf16)] * 3 + [((rows, width), bf16)]
        + [((ff, width), bf16)] * last_k + [((ff + rows, width), bf16)] * (last_k - 1)
        + [((fold_ff + rows, width), bf16)],
        [pltpu.VMEM((hidden_ff, width), bf16)] * 2,
    )
    out_half, x0, y0, d0, gf0 = rest[:5]
    send_x, send_d = rest[5:5 + last_k], rest[5 + last_k:]
    outs_r = [out_weight] + [col_send(out_weight if k < last_k else out_half, k) for k in peers()]
    outs_r.append(pair_send(outs_r[last_k]))
    xs = [x0] + [col_send(send_x[k - 1], k) for k in peers()]
    ys = [y0] + [pair_send(x) for k, x in enumerate(xs) if k]
    downs = [d0] + [col_send(send_d[k - 1], k) for k in peers()]
    gfs = [gf0] + downs[1:]
    gfs_o = [row_send(a) for a in gfs]
    downs.append(pair_send(downs[last_k]))
    n_out = n_col + 1

    def mixer(inf, sg, taps, *refs):
        own, oth, w = refs[:n_col], refs[n_col:2 * n_col], refs[2 * n_col:3 * n_col]
        tok, gains, mixed, mix3, n1 = refs[3 * n_col:]
        total = jnp.zeros((group, 1), f32)
        for k in K:
            cols = slice(k * width, (k + 1) * width)
            tok[:rows, cols] = own[k][...]
            tok[rows:, cols] = oth[k][...]
            for i in range(2):
                gain = w[k][width:, :width].astype(f32)[3 * i:3 * i + 3]
                gains[i:i + 1, cols] = gain[0:1] + gain[1:2] + gain[2:3]
            part = tok[:, cols]
            total = total + jnp.sum(part * part, axis=1, keepdims=True)
        scale = lax.rsqrt(total / model + epsilon)
        acc = jnp.zeros((group, 3 * lanes), f32)
        for k in K:
            cols = slice(k * width, (k + 1) * width)
            normed = (tok[:, cols] * scale * gains[0:1, cols]).astype(bf16)
            if k == 0:
                n1[...] = normed
            acc = acc + dot(normed, w[k][:width], 1, 0)
        mix3[...] = acc
        one, two = masks(sg[...], inf[1], rows, group)
        product = acc[:, :lanes] * acc[:, 2 * lanes:]
        conv = (
            taps[2:3] * product
            + taps[1:2] * (pltpu.roll(product, 1, 0) * one)
            + taps[0:1] * (pltpu.roll(product, 2, 0) * two)
        )
        mixed[...] = (acc[:, lanes:2 * lanes] * conv).astype(bf16)

    tok, gains, mixed, mix3, n1 = call(
        mixer, info, [seg, conv_taps] + toks + toks_o + w_in,
        [
            ((group, model), f32), ((8, model), f32), ((group, lanes), bf16),
            ((group, 3 * lanes), f32), ((group, width), bf16),
        ],
    )
    mixeds = [mixed] + [col_send(mixed, k) for k in peers()]

    def outproj(inf, *refs):
        mo, wr = refs[:n_col], refs[n_col:n_col + n_out]
        hp, ms = refs[n_col + n_out:]
        cc, p = inf[0], inf[2]
        for k in K:
            ms[:, pl.ds(pl.multiple_of((cc ^ k) * lanes, lanes), lanes)] = mo[k][...]
        near = pl.ds(pl.multiple_of(p * ho, ho), ho)
        away = pl.ds(pl.multiple_of((1 - p) * ho, ho), ho)
        for k in K:
            cols = slice(k * width, (k + 1) * width)
            if k < last_k:
                hp[:, cols] = dot(ms[...], wr[k][...], 1, 0)
            else:
                hp[:, cols] = dot(ms[:, near], wr[k][...], 1, 0) + dot(ms[:, away], wr[k + 1][...], 1, 0)

    hp, = call(
        outproj, info, mixeds + outs_r, [((group, model), f32)],
        [pltpu.VMEM((group, span), bf16)],
    )
    hp_o = row_send(hp)

    def ffn_in(inf, tk, gn, mine, other, *refs):
        x, y = refs[:n_col], refs[n_col:2 * n_col]
        hidden, gp_out, up_out, act_out, n2 = refs[2 * n_col:]
        p = inf[2]
        total = jnp.zeros((group, 1), f32)
        for k in K:
            cols = slice(k * width, (k + 1) * width)
            swapped = jnp.concatenate([other[rows:, cols], other[:rows, cols]], axis=0)
            h = tk[:, cols] + (mine[:, cols] + swapped)
            hidden[:, cols] = h
            total = total + jnp.sum(h * h, axis=1, keepdims=True)
        scale = lax.rsqrt(total / model + epsilon)
        ax = jnp.zeros((ff, group), f32)
        ay = jnp.zeros((ff, group), f32)
        for k in K:
            cols = slice(k * width, (k + 1) * width)
            normed = (hidden[:, cols] * scale * gn[1:2, cols]).astype(bf16)
            if k == 0:
                n2[...] = normed
            ax = ax + dot(x[k][...], normed, 1, 1)
            ay = ay + dot(y[k][...], normed, 1, 1)
        gp = jnp.where(p == 0, ax, ay)
        up = jnp.where(p == 0, ay, ax)
        gp_out[...] = gp
        up_out[...] = up
        act_out[...] = (gp * jax.nn.sigmoid(gp) * up).astype(bf16)

    hidden, gate_proj, up_proj, act, n2 = call(
        ffn_in, info, [tok, gains, hp, hp_o] + xs + ys,
        [
            ((group, model), f32), ((ff, group), f32), ((ff, group), f32), ((ff, group), bf16),
            ((group, width), bf16),
        ],
        flops=2 * 10**9,
    )

    cut = 3 * ff // 2

    cut = 3 * ff // 2

    def ffn_back(inf, gpr, upr, act_ref, n2r, *refs):
        go, gx = refs[:n_col], refs[n_col:2 * n_col]
        dn = refs[2 * n_col:3 * n_col + 1]
        piece, chunk_a, chunk_b, gf, chunk = refs[3 * n_col + 1:]
        p = inf[2]
        ga = jnp.zeros((ff, group), f32)
        for k in K:
            skip = go[k].shape[0] - rows
            gf[k, :rows] = go[k][skip:]
            gf[k, rows:] = gx[k][skip:]
            if k < last_k:
                ga = ga + dot(dn[k][:ff], gf[k], 1, 1)
            else:
                near = gf[k, :, pl.ds(pl.multiple_of(p * hw, hw), hw)]
                away = gf[k, :, pl.ds(pl.multiple_of((1 - p) * hw, hw), hw)]
                for g, d in ((near, dn[k]), (away, dn[k + 1])):
                    top = dot(d[:fold_ff, :hw], g, 1, 1)
                    ga = ga + jnp.concatenate([top, dot(d[:fold_ff, hw:], g, 1, 1)], axis=0)
        gp, up = gpr[...], upr[...]
        sig = jax.nn.sigmoid(gp)
        piece[:ff] = act_ref[...]
        piece[ff:2 * ff] = (ga * up * sig * (1.0 + gp * (1.0 - sig))).astype(bf16)
        piece[2 * ff:] = (ga * gp * sig).astype(bf16)
        chunk[:ff] = dot(act_ref[...], gf[0], 1, 0).astype(bf16)
        chunk[ff:] = dot(piece[ff:], n2r[...], 1, 0).astype(bf16)
        chunk_a[...] = chunk[:cut]
        chunk_b[...] = chunk[cut:]

    piece0, chunk_a, chunk_b = call(
        ffn_back, info, [gate_proj, up_proj, act, n2] + gfs + gfs_o + downs,
        [((3 * ff, group), bf16), ((cut, width), bf16), ((3 * ff - cut, width), bf16)],
        [pltpu.VMEM((n_col, group, width), bf16), pltpu.VMEM((3 * ff, width), bf16)],
        flops=2 * 10**9,
    )

    def ffn_part(inf, pc, *refs):
        x, y = refs[:n_col], refs[n_col:2 * n_col]
        mine, sent = refs[2 * n_col:]
        gg, gu = pc[ff:2 * ff], pc[2 * ff:]
        a = jnp.where(inf[2] == 0, gg, gu).T
        b = jnp.where(inf[2] == 0, gu, gg).T
        for k in K:
            cols = slice(k * width, (k + 1) * width)
            part = dot(a, x[k][...], 1, 0) + dot(b, y[k][...], 1, 0)
            mine[:, cols] = part[:rows]
            sent[:, cols] = part[rows:].astype(bf16)

    mine2, sent2 = call(
        ffn_part, info, [piece0] + xs + ys,
        [((rows, model), f32), ((rows, model), bf16)], flops=10**9,
    )

    def fold(which):
        def body(inf, mn, came, act_in, gn, own, rs, *outs):
            total = mn[...] + came[...].astype(f32)
            rowsum = jnp.sum(total * act_in[:rows] * gn[which:which + 1], axis=1, keepdims=True)
            line = jnp.broadcast_to(rowsum, (rows, rows)).T[:16]
            high = line.astype(bf16)
            low = (line - high.astype(f32)).astype(bf16)
            own[...] = total[:, :width]
            rs[...] = jnp.broadcast_to(rowsum, (rows, 128))
            for k in peers():
                outs[k - 1][:rows] = total[:, k * width:(k + 1) * width].astype(bf16)
                outs[k - 1][rows:] = jnp.zeros((16, width), bf16)
                outs[k - 1][rows:, :rows] = high
                outs[k - 1][rows:, width - rows:] = low

        return body

    fold_outs = [((rows, width), f32), ((rows, 128), f32)] + [((rows + 16, width), bf16)] * (n_col - 1)

    def unfold(own, rs, came):
        total, line = own[...], jnp.zeros((16, rows), f32)
        for ref in came:
            total = total + ref[:rows].astype(f32)
            line = line + ref[rows:, :rows].astype(f32) + ref[rows:, width - rows:].astype(f32)
        return total, rs[:, :1] + jnp.broadcast_to(line[:1], (rows, rows)).T[:, :1]

    came2 = row_send(sent2)
    own2, rs2, *send2 = call(fold(1), info, [mine2, came2, hidden, gains], fold_outs)
    got2 = [col_send(s, k + 1) for k, s in enumerate(send2)]

    def mid(inf, own, rs, hid_ref, gn, og, *refs):
        came, (grad_mid, mix, gain) = refs[:n_col - 1], refs[n_col - 1:]
        total, mean = unfold(own, rs, came)
        full = hid_ref[:rows]
        scale = lax.rsqrt(jnp.sum(full * full, axis=1, keepdims=True) / model + epsilon)
        hid = hid_ref[:rows, :width]
        gm = og[...] + scale * (gn[1:2, :width] * total) - hid * (scale * scale * scale) * (mean / model)
        grad_mid[...] = gm
        mix[...] = gm.astype(bf16)
        gain[...] = jnp.broadcast_to(jnp.sum(total * hid * scale, axis=0, keepdims=True), (8, width))

    grad_mid, gmix0, gain_two = call(
        mid, info, [own2, rs2, hidden, gains, out_grad] + got2,
        [((rows, width), f32), ((rows, width), bf16), ((8, width), f32)],
    )
    gmix = [gmix0] + [col_send(gmix0, k) for k in peers()]
    gmix_o = [row_send(m) for m in gmix]

    pieces = [piece0] + [col_send(piece0, k) for k in peers()]

    def ffn_grad(inf, pc, gfa, gfb, n2r, out_a, out_b, gf, out):
        gf[:rows] = gfa[...]
        gf[rows:] = gfb[...]
        out[:ff] = dot(pc[:ff], gf[...], 1, 0).astype(bf16)
        out[ff:] = dot(pc[ff:], n2r[...], 1, 0).astype(bf16)
        out_a[...] = out[:cut]
        out_b[...] = out[cut:]

    chunks = [chunk_a, chunk_b]
    for k in peers():
        chunk_a, chunk_b = call(
            ffn_grad, info, [pieces[k], gf0, gfs_o[0], n2],
            [((cut, width), bf16), ((3 * ff - cut, width), bf16)],
            [pltpu.VMEM((group, width), bf16), pltpu.VMEM((3 * ff, width), bf16)],
        )
        chunks += [chunk_a, chunk_b]

    def mixer_back(inf, sg, taps, m3, *refs):
        go, gx = refs[:n_col], refs[n_col:2 * n_col]
        w = refs[2 * n_col:2 * n_col + n_out]
        wi = refs[2 * n_col + n_out:][:n_col]
        trip_t, mine, sent, tg = refs[3 * n_col + n_out:]
        cc, p = inf[0], inf[2]
        inside = lax.rem(cc * lanes, ho)
        at = pl.ds(pl.multiple_of(inside, lanes), lanes)
        here = (cc * lanes >= ho) == (p == 1)
        gm = jnp.zeros((group, lanes), f32)
        for k in K:
            if k < last_k:
                wk = w[k][pl.ds(pl.multiple_of(cc * lanes, lanes), lanes), :]
            else:
                wk = jnp.where(here, w[k][at, :], w[k + 1][at, :])
            gm = gm + dot(jnp.concatenate([go[k][...], gx[k][...]], axis=0), wk, 1, 1)
        one, two = masks(sg[...], inf[1], rows, group)
        gate_in, gate_out, carried = m3[:, :lanes], m3[:, lanes:2 * lanes], m3[:, 2 * lanes:]
        product = gate_in * carried
        back_one = pltpu.roll(product, 1, 0) * one
        back_two = pltpu.roll(product, 2, 0) * two
        conv = taps[2:3] * product + taps[1:2] * back_one + taps[0:1] * back_two
        gc = gm * gate_out
        gpr = (
            taps[2:3] * gc
            + taps[1:2] * pltpu.roll(gc * one, group - 1, 0)
            + taps[0:1] * pltpu.roll(gc * two, group - 2, 0)
        )
        tg[...] = jnp.zeros((8, lanes), f32)
        tg[0:1] = jnp.sum(gc * back_two, axis=0, keepdims=True)
        tg[1:2] = jnp.sum(gc * back_one, axis=0, keepdims=True)
        tg[2:3] = jnp.sum(gc * product, axis=0, keepdims=True)
        triple = jnp.concatenate([gpr * carried, gm * conv, gpr * gate_in], axis=1)
        trip_t[...] = triple.T.astype(bf16)
        low = triple.astype(bf16)
        for k in K:
            cols = slice(k * width, (k + 1) * width)
            part = dot(low, wi[k][:width], 1, 1)
            mine[:, cols] = part[:rows]
            sent[:, cols] = part[rows:].astype(bf16)

    trip0, mine1, sent1, taps_grad = call(
        mixer_back, info, [seg, conv_taps, mix3] + gmix + gmix_o + outs_r + w_in,
        [((3 * lanes, group), bf16), ((rows, model), f32), ((rows, model), bf16), ((8, lanes), f32)],
    )
    trips = [trip0] + [col_send(trip0, k) for k in peers()]

    def mix_grad(inf, n1r, ga, gb, *refs):
        count = len(refs[:-1]) // 3
        gm = refs[-1]
        gm[:rows] = ga[...]
        gm[rows:] = gb[...]
        for tr, mx, out in zip(refs[:count], refs[count:2 * count], refs[2 * count:-1]):
            out[:3 * lanes] = dot(tr[...], n1r[...], 1, 0).astype(bf16)
            out[3 * lanes:] = dot(mx[...].T, gm[...], 1, 0).astype(bf16)

    for part in (slice(0, 1), slice(1, n_col)):
        chunks += call(
            mix_grad, info, [n1, gmix[0], gmix_o[0]] + trips[part] + mixeds[part],
            [((4 * lanes, width), bf16)] * len(trips[part]), [pltpu.VMEM((group, width), bf16)],
        )

    came1 = row_send(sent1)
    own1, rs1, *send1 = call(fold(0), info, [mine1, came1, tok, gains], fold_outs)
    got1 = [col_send(s, k + 1) for k, s in enumerate(send1)]

    def last(inf, own, rs, tk, gn, gmid, gtwo, *refs):
        came, (out, gain) = refs[:n_col - 1], refs[n_col - 1:]
        total, mean = unfold(own, rs, came)
        full = tk[:rows]
        scale = lax.rsqrt(jnp.sum(full * full, axis=1, keepdims=True) / model + epsilon)
        part = tk[:rows, :width]
        out[...] = gmid[...] + scale * (gn[0:1, :width] * total) - part * (scale * scale * scale) * (mean / model)
        gain[...] = gtwo[...]
        gain[0:1] = jnp.sum(total * part * scale, axis=0, keepdims=True)

    in_grad, gain_pair = call(
        last, info, [own1, rs1, tok, gains, grad_mid, gain_two] + got1,
        [((rows, width), f32), ((8, width), f32)],
    )

    gain_came = row_send(gain_pair)

    def ffn_out(inf, dw, hid, ga, gb, tg, *refs):
        pcs, (mine, sent, small) = refs[:n_col], refs[n_col:]
        acc = jnp.zeros((group, width), f32)
        for k in K:
            at = pl.ds(pl.multiple_of((inf[0] ^ k) * ff, 32), ff)
            acc = acc + dot(pcs[k][:ff].T, dw[at, :], 1, 0)
        mine[...] = acc[:rows] + hid[:rows, :width]
        sent[...] = acc[rows:]
        wide = jnp.concatenate([tg[...], jnp.zeros((8, width - lanes), f32)], axis=1) if width > lanes else tg[...]
        small[...] = jnp.concatenate([ga[...] + gb[...], wide], axis=0).astype(bf16)

    out_mine, out_sent, small = call(
        ffn_out, info, [down_weight, hidden, gain_pair, gain_came, taps_grad] + pieces,
        [((rows, width), f32)] * 2 + [((16, width), bf16)],
    )
    out_came = row_send(out_sent)

    chunks.append(small)
    sums = dp_sums(chunks)

    def place_down(inf, *refs):
        parts, (oa, ob, down, out) = refs[:2 * n_col], refs[2 * n_col:]
        out[...] = oa[...] + ob[...]
        for k in K:
            at = pl.ds(pl.multiple_of((inf[0] ^ k) * ff, 32), ff)
            down[at, :] = jnp.where(inf[3] == 1, parts[2 * k + 1][:ff], parts[2 * k][:ff]).astype(f32)

    down_sum, block_out = call(
        place_down, info, [x for s in sums[:2 * n_col:2] for x in s] + [out_mine, out_came],
        [((hidden_ff, width), f32), ((rows, width), f32)],
    )

    def ffn_place(inf, *refs):
        parts, (gate, up, gt, ut) = refs[:4 * n_col], refs[4 * n_col:]
        far = inf[3] == 1
        for k in K:
            ha, ca, hb, cb = parts[4 * k:4 * k + 4]
            at = (inf[0] ^ k) * ff
            near = cut - ff
            gt[pl.ds(pl.multiple_of(at, 32), near), :] = jnp.where(far, ca[ff:cut], ha[ff:cut])
            gt[pl.ds(pl.multiple_of(at + near, 32), ff - near), :] = jnp.where(far, cb[:ff - near], hb[:ff - near])
            ut[pl.ds(pl.multiple_of(at, 32), ff), :] = jnp.where(far, cb[ff - near:cut], hb[ff - near:cut])
        gate[...] = gt[...].T.astype(f32)
        up[...] = ut[...].T.astype(f32)

    gate_sum, up_sum = call(
        ffn_place, info, [x for s in sums[:2 * n_col] for x in s],
        [((width, hidden_ff), f32)] * 2, [pltpu.VMEM((hidden_ff, width), bf16)] * 2,
    )

    def mix_place(inf, *refs):
        held_refs, came_refs = refs[:n_col], refs[n_col + 1:2 * n_col + 1]
        win, wout, g1, g2, tg = refs[2 * n_col + 2:]
        far = inf[3] == 1
        small = jnp.where(far, refs[2 * n_col + 1][...], refs[n_col][...]).astype(f32)
        g1[...] = small[0:1]
        g2[...] = small[1:2]
        tg[...] = small[8:11, :lanes]
        for k in K:
            at = pl.ds(pl.multiple_of((inf[0] ^ k) * lanes, lanes), lanes)
            for t in range(4):
                rr = slice(t * lanes, (t + 1) * lanes)
                got = jnp.where(far, came_refs[k][rr], held_refs[k][rr])
                if t < 3:
                    win[t, :, at] = got.T.astype(f32)
                else:
                    wout[at, :] = got.astype(f32)

    in_sum, out_sum, small_one, small_two, small_taps = call(
        mix_place, info, [s[0] for s in sums[2 * n_col:]] + [s[1] for s in sums[2 * n_col:]],
        [((3, width, span), f32), ((span, width), f32)] + [((1, width), f32)] * 2 + [((3, lanes), f32)],
    )
    return (
        block_out,
        in_grad,
        small_one.reshape(width),
        jnp.transpose(in_sum, (1, 0, 2)),
        small_taps,
        out_sum,
        small_two.reshape(width),
        gate_sum,
        up_sum,
        down_sum,
    )


def solution(mesh):
    token = P(("dp", "row"), "col")
    feature, tap = P("col"), P(None, ("row", "col"))
    split_in, split_up, split_down = P("col", None, "row"), P("col", "row"), P("row", "col")
    weights = (feature, split_in, tap, split_down, feature, split_up, split_up, split_down)
    in_specs = (token, P("dp"), *weights, token)
    out_specs = (token, token, *weights)

    return jax.shard_map(per_device, mesh=mesh, in_specs=in_specs, out_specs=out_specs, check_vma=False)
```

```python
import jax
import jax.numpy as jnp
from jax import lax
from jax.experimental import pallas as pl
from jax.experimental.pallas import tpu as pltpu
from jax.sharding import PartitionSpec as P


epsilon = 1e-05
f32 = jnp.float32
bf16 = jnp.bfloat16


SMEM = pl.BlockSpec(memory_space=pltpu.SMEM)
VMEM = pl.BlockSpec(memory_space=pltpu.VMEM)


def dot(left, right, ldim, rdim):
    return lax.dot_general(left, right, (((ldim,), (rdim,)), ((), ())), preferred_element_type=f32)


def call(body, info, args, outs, scratch=(), flops=10**8):
    size = sum(a.size * a.dtype.itemsize for a in args)
    return pl.pallas_call(
        body,
        out_shape=[jax.ShapeDtypeStruct(s, t) for s, t in outs],
        in_specs=[SMEM] + [VMEM] * len(args),
        out_specs=[VMEM] * len(outs),
        scratch_shapes=list(scratch),
        compiler_params=pltpu.CompilerParams(vmem_limit_bytes=56 * 1024 * 1024),
        cost_estimate=pl.CostEstimate(flops=flops, bytes_accessed=size, transcendentals=0),
    )(info, *args)


def peers():
    n = lax.axis_size("col")
    assert n & (n - 1) == 0
    return range(1, n)


def col_send(piece, k):
    n = lax.axis_size("col")
    return lax.ppermute(piece, "col", [(i, i ^ k) for i in range(n)])


def row_send(piece):
    n = lax.axis_size("row")
    assert n == 2
    return lax.ppermute(piece, "row", [(i, (i + 1) % n) for i in range(n)])


def pair_send(piece):
    n = lax.axis_size("dp")
    assert n % 2 == 0
    return lax.ppermute(piece, "dp", [(i, i ^ 1) for i in range(n)])


def add_to(held, came, kind):
    return (held.astype(f32) + came.astype(f32)).astype(kind)


def line_sum(part):
    n = lax.axis_size("dp")
    me = lax.axis_index("dp")
    half = n // 2
    kind = part.dtype
    held = part
    for s in range(half - 1):
        came = lax.ppermute(held, "dp", [(s, s + 1), (n - 1 - s, n - 2 - s)])
        held = add_to(held, came, kind)
    came = lax.ppermute(held, "dp", [(half - 1, half), (half, half - 1)])
    held = add_to(held, came, kind)
    came = held
    for s in range(half - 1):
        came = lax.ppermute(held, "dp", [(half - 1 - s, half - 2 - s), (half + s, half + 1 + s)])
        if s < half - 2:
            got = (me == half - 2 - s) | (me == half + 1 + s)
            held = jnp.where(got, came, held)
    return held, came


LAG = 3


def dp_sums(chunks):
    n = lax.axis_size("dp")
    if n != 4:
        return [line_sum(g) for g in chunks]
    two = lax.axis_size("row")
    ends = [(i, i ^ 1) for i in range(n)]
    inner = [(a * two + r, b * two + r) for a, b in ((1, 2), (2, 1)) for r in range(two)]
    inner += [(a * two + r, a * two + (r + 1) % two) for a in (0, 3) for r in range(two)]
    far = far_end() == 1
    held, came_mid, totals = [], [], []
    for i in range(len(chunks) + LAG):
        t = None
        if i >= LAG:
            t = add_to(held[i - LAG], came_mid[i - LAG], bf16)
        if i >= len(chunks):
            sent = t
        else:
            g = chunks[i]
            sent = g
            if t is not None:
                size = max(g.shape[0], t.shape[0])
                sent = jnp.where(
                    far,
                    jnp.pad(g, ((0, size - g.shape[0]), (0, 0))),
                    jnp.pad(t, ((0, size - t.shape[0]), (0, 0))),
                )
        came = lax.ppermute(sent, "dp", ends)
        if i < len(chunks):
            h = add_to(g, came[:g.shape[0]], bf16)
            held.append(h)
            came_mid.append(lax.ppermute(h, ("dp", "row"), inner))
        if i >= LAG:
            totals.append((sent, came))
    return totals


def far_end():
    n = lax.axis_size("dp")
    me = lax.axis_index("dp")
    return (((me == 0) | (me == n - 1)) & (n > 2)).astype(jnp.int32)


def masks(seg, r, rows, group):
    wide = jnp.broadcast_to(seg, (group, 128))
    wide = jnp.where(r == 0, wide, pltpu.roll(wide, rows, 0))
    place = lax.broadcasted_iota(jnp.int32, (group, 128), 0) + r * rows
    place = jnp.where(place >= group, place - group, place)
    one = jnp.where((wide == pltpu.roll(wide, 1, 0)) & (place >= 1), 1.0, 0.0)
    two = jnp.where((wide == pltpu.roll(wide, 2, 0)) & (place >= 2), 1.0, 0.0)
    return one, two


def per_device(
    tokens,
    segment_ids,
    norm_gain,
    in_weight,
    conv_taps,
    out_weight,
    ffn_gain,
    gate_weight,
    up_weight,
    down_weight,
    out_grad,
):
    rows, width = tokens.shape
    n_col = lax.axis_size("col")
    n_row = lax.axis_size("row")
    c = lax.axis_index("col")
    r = lax.axis_index("row")
    model = width * n_col
    group = rows * n_row
    span = in_weight.shape[2]
    lanes = span // n_col
    hidden_ff = gate_weight.shape[1]
    ff = hidden_ff // n_col
    K = range(n_col)
    hw = width // 2
    ho = span // 2
    info = jnp.stack([c, r, lax.axis_index("dp") % 2, far_end()]).astype(jnp.int32)
    seg = segment_ids[:, None]
    in_t = jnp.transpose(in_weight, (1, 0, 2))

    toks = [tokens] + [col_send(tokens, k) for k in peers()]
    toks_o = [row_send(p) for p in toks]

    def prep_first(inf, ng, fg, w, *outs):
        cc = inf[0]
        parts = []
        for g in (ng[...], fg[...]):
            for _ in range(3):
                piece = g.astype(bf16).astype(f32)
                parts.append(piece)
                g = g - piece
        at = lax.broadcasted_iota(jnp.int32, (16, width), 0)
        lines = jnp.zeros((16, width), f32)
        for i, piece in enumerate(parts):
            lines = jnp.where(at == i, jnp.broadcast_to(piece, (16, width)), lines)
        lines = lines.astype(bf16)
        for k in K:
            at = pl.multiple_of((cc ^ k) * lanes, lanes)
            for t in range(3):
                outs[k][:width, t * lanes:(t + 1) * lanes] = w[t, :, pl.ds(at, lanes)]
            outs[k][width:] = jnp.zeros((16, 3 * lanes), bf16)
            outs[k][width:, :width] = lines

    w_in = call(
        prep_first, info, [norm_gain[None], ffn_gain[None], in_t],
        [((width + 16, 3 * lanes), bf16)] * n_col,
    )
    w_in = [w_in[0]] + [col_send(w_in[k], k) for k in peers()]

    last_k = n_col - 1
    fold_ff = ff // 2

    def prep_rest(inf, ow, gw, uw, dw, og, oh, x0, y0, d0, gf, *outs):
        gt, ut = outs[-2:]
        cc, p = inf[0], inf[2]
        oh[...] = ow[pl.ds(pl.multiple_of(p * ho, ho), ho), :]
        gt[...] = gw[...].T
        ut[...] = uw[...].T
        gf[...] = og[...].astype(bf16)
        for k in K:
            at = pl.ds(pl.multiple_of((cc ^ k) * ff, 32), ff)
            x = jnp.where(p == 0, gt[at, :], ut[at, :])
            if k == 0:
                x0[...] = x
                y0[...] = jnp.where(p == 0, ut[at, :], gt[at, :])
                d0[...] = dw[at, :]
            else:
                outs[k - 1][...] = x
                dn = outs[last_k + k - 1]
                if k < last_k:
                    dn[:ff] = dw[at, :]
                    dn[ff:] = gf[...]
                else:
                    part = dw[at, pl.ds(pl.multiple_of(p * hw, hw), hw)]
                    dn[:fold_ff, :hw] = part[:fold_ff]
                    dn[:fold_ff, hw:] = part[fold_ff:]
                    dn[fold_ff:] = gf[...]

    rest = call(
        prep_rest, info, [out_weight, gate_weight, up_weight, down_weight, out_grad],
        [((ho, width), bf16)] + [((ff, width), bf16)] * 3 + [((rows, width), bf16)]
        + [((ff, width), bf16)] * last_k + [((ff + rows, width), bf16)] * (last_k - 1)
        + [((fold_ff + rows, width), bf16)],
        [pltpu.VMEM((hidden_ff, width), bf16)] * 2,
    )
    out_half, x0, y0, d0, gf0 = rest[:5]
    send_x, send_d = rest[5:5 + last_k], rest[5 + last_k:]
    outs_r = [out_weight] + [col_send(out_weight if k < last_k else out_half, k) for k in peers()]
    outs_r.append(pair_send(outs_r[last_k]))
    xs = [x0] + [col_send(send_x[k - 1], k) for k in peers()]
    ys = [y0] + [pair_send(x) for k, x in enumerate(xs) if k]
    downs = [d0] + [col_send(send_d[k - 1], k) for k in peers()]
    gfs = [gf0] + downs[1:]
    gfs_o = [row_send(a) for a in gfs]
    downs.append(pair_send(downs[last_k]))
    n_out = n_col + 1

    def mixer(inf, sg, taps, *refs):
        own, oth, w = refs[:n_col], refs[n_col:2 * n_col], refs[2 * n_col:3 * n_col]
        tok, gains, mixed, mix3, n1 = refs[3 * n_col:]
        total = jnp.zeros((group, 1), f32)
        for k in K:
            cols = slice(k * width, (k + 1) * width)
            tok[:rows, cols] = own[k][...]
            tok[rows:, cols] = oth[k][...]
            for i in range(2):
                gain = w[k][width:, :width].astype(f32)[3 * i:3 * i + 3]
                gains[i:i + 1, cols] = gain[0:1] + gain[1:2] + gain[2:3]
            part = tok[:, cols]
            total = total + jnp.sum(part * part, axis=1, keepdims=True)
        scale = lax.rsqrt(total / model + epsilon)
        acc = jnp.zeros((group, 3 * lanes), f32)
        for k in K:
            cols = slice(k * width, (k + 1) * width)
            normed = (tok[:, cols] * scale * gains[0:1, cols]).astype(bf16)
            if k == 0:
                n1[...] = normed
            acc = acc + dot(normed, w[k][:width], 1, 0)
        mix3[...] = acc
        one, two = masks(sg[...], inf[1], rows, group)
        product = acc[:, :lanes] * acc[:, 2 * lanes:]
        conv = (
            taps[2:3] * product
            + taps[1:2] * (pltpu.roll(product, 1, 0) * one)
            + taps[0:1] * (pltpu.roll(product, 2, 0) * two)
        )
        mixed[...] = (acc[:, lanes:2 * lanes] * conv).astype(bf16)

    tok, gains, mixed, mix3, n1 = call(
        mixer, info, [seg, conv_taps] + toks + toks_o + w_in,
        [
            ((group, model), f32), ((8, model), f32), ((group, lanes), bf16),
            ((group, 3 * lanes), f32), ((group, width), bf16),
        ],
    )
    mixeds = [mixed] + [col_send(mixed, k) for k in peers()]

    def outproj(inf, *refs):
        mo, wr = refs[:n_col], refs[n_col:n_col + n_out]
        hp, ms = refs[n_col + n_out:]
        cc, p = inf[0], inf[2]
        for k in K:
            ms[:, pl.ds(pl.multiple_of((cc ^ k) * lanes, lanes), lanes)] = mo[k][...]
        near = pl.ds(pl.multiple_of(p * ho, ho), ho)
        away = pl.ds(pl.multiple_of((1 - p) * ho, ho), ho)
        for k in K:
            cols = slice(k * width, (k + 1) * width)
            if k < last_k:
                hp[:, cols] = dot(ms[...], wr[k][...], 1, 0)
            else:
                hp[:, cols] = dot(ms[:, near], wr[k][...], 1, 0) + dot(ms[:, away], wr[k + 1][...], 1, 0)

    hp, = call(
        outproj, info, mixeds + outs_r, [((group, model), f32)],
        [pltpu.VMEM((group, span), bf16)],
    )
    hp_o = row_send(hp)

    def ffn_in(inf, tk, gn, mine, other, *refs):
        x, y = refs[:n_col], refs[n_col:2 * n_col]
        hidden_out, gp_out, up_out, act_out, n2, hidden = refs[2 * n_col:]
        p = inf[2]
        total = jnp.zeros((group, 1), f32)
        for k in K:
            cols = slice(k * width, (k + 1) * width)
            swapped = jnp.concatenate([other[rows:, cols], other[:rows, cols]], axis=0)
            h = tk[:, cols] + (mine[:, cols] + swapped)
            hidden[:, cols] = h
            total = total + jnp.sum(h * h, axis=1, keepdims=True)
        hidden_out[...] = hidden[:rows]
        scale = lax.rsqrt(total / model + epsilon)
        ax = jnp.zeros((ff, group), f32)
        ay = jnp.zeros((ff, group), f32)
        for k in K:
            cols = slice(k * width, (k + 1) * width)
            normed = (hidden[:, cols] * scale * gn[1:2, cols]).astype(bf16)
            if k == 0:
                n2[...] = normed
            ax = ax + dot(x[k][...], normed, 1, 1)
            ay = ay + dot(y[k][...], normed, 1, 1)
        gp = jnp.where(p == 0, ax, ay)
        up = jnp.where(p == 0, ay, ax)
        gp_out[...] = gp
        up_out[...] = up
        act_out[...] = (gp * jax.nn.sigmoid(gp) * up).astype(bf16)

    hidden, gate_proj, up_proj, act, n2 = call(
        ffn_in, info, [tok, gains, hp, hp_o] + xs + ys,
        [
            ((rows, model), f32), ((ff, group), f32), ((ff, group), f32), ((ff, group), bf16),
            ((group, width), bf16),
        ],
        [pltpu.VMEM((group, model), f32)],
        flops=2 * 10**9,
    )

    cut = 3 * ff // 2

    cut = 3 * ff // 2

    def ffn_back(inf, gpr, upr, act_ref, n2r, *refs):
        go, gx = refs[:n_col], refs[n_col:2 * n_col]
        dn = refs[2 * n_col:3 * n_col + 1]
        piece, chunk_a, chunk_b, gf, chunk = refs[3 * n_col + 1:]
        p = inf[2]
        ga = jnp.zeros((ff, group), f32)
        for k in K:
            skip = go[k].shape[0] - rows
            gf[k, :rows] = go[k][skip:]
            gf[k, rows:] = gx[k][skip:]
            if k < last_k:
                ga = ga + dot(dn[k][:ff], gf[k], 1, 1)
            else:
                near = gf[k, :, pl.ds(pl.multiple_of(p * hw, hw), hw)]
                away = gf[k, :, pl.ds(pl.multiple_of((1 - p) * hw, hw), hw)]
                for g, d in ((near, dn[k]), (away, dn[k + 1])):
                    top = dot(d[:fold_ff, :hw], g, 1, 1)
                    ga = ga + jnp.concatenate([top, dot(d[:fold_ff, hw:], g, 1, 1)], axis=0)
        gp, up = gpr[...], upr[...]
        sig = jax.nn.sigmoid(gp)
        piece[:ff] = (ga * up * sig * (1.0 + gp * (1.0 - sig))).astype(bf16)
        piece[ff:] = (ga * gp * sig).astype(bf16)
        chunk[:ff] = dot(act_ref[...], gf[0], 1, 0).astype(bf16)
        chunk[ff:] = dot(piece[...], n2r[...], 1, 0).astype(bf16)
        chunk_a[...] = chunk[:cut]
        chunk_b[...] = chunk[cut:]

    piece0, chunk_a, chunk_b = call(
        ffn_back, info, [gate_proj, up_proj, act, n2] + gfs + gfs_o + downs,
        [((2 * ff, group), bf16), ((cut, width), bf16), ((3 * ff - cut, width), bf16)],
        [pltpu.VMEM((n_col, group, width), bf16), pltpu.VMEM((3 * ff, width), bf16)],
        flops=2 * 10**9,
    )

    def ffn_part(inf, pc, *refs):
        x, y = refs[:n_col], refs[n_col:2 * n_col]
        mine, sent = refs[2 * n_col:]
        gg, gu = pc[:ff], pc[ff:]
        a = jnp.where(inf[2] == 0, gg, gu).T
        b = jnp.where(inf[2] == 0, gu, gg).T
        for k in K:
            cols = slice(k * width, (k + 1) * width)
            part = dot(a, x[k][...], 1, 0) + dot(b, y[k][...], 1, 0)
            mine[:, cols] = part[:rows]
            sent[:, cols] = part[rows:].astype(bf16)

    mine2, sent2 = call(
        ffn_part, info, [piece0] + xs + ys,
        [((rows, model), f32), ((rows, model), bf16)], flops=10**9,
    )

    def fold(which):
        def body(inf, mn, came, act_in, gn, own, rs, *outs):
            total = mn[...] + came[...].astype(f32)
            rowsum = jnp.sum(total * act_in[:rows] * gn[which:which + 1], axis=1, keepdims=True)
            line = jnp.broadcast_to(rowsum, (rows, rows)).T[:16]
            high = line.astype(bf16)
            low = (line - high.astype(f32)).astype(bf16)
            own[...] = total[:, :width]
            rs[...] = jnp.broadcast_to(rowsum, (rows, 128))
            for k in peers():
                outs[k - 1][:rows] = total[:, k * width:(k + 1) * width].astype(bf16)
                outs[k - 1][rows:] = jnp.zeros((16, width), bf16)
                outs[k - 1][rows:, :rows] = high
                outs[k - 1][rows:, width - rows:] = low

        return body

    fold_outs = [((rows, width), f32), ((rows, 128), f32)] + [((rows + 16, width), bf16)] * (n_col - 1)

    def unfold(own, rs, came):
        total, line = own[...], jnp.zeros((16, rows), f32)
        for ref in came:
            total = total + ref[:rows].astype(f32)
            line = line + ref[rows:, :rows].astype(f32) + ref[rows:, width - rows:].astype(f32)
        return total, rs[:, :1] + jnp.broadcast_to(line[:1], (rows, rows)).T[:, :1]

    came2 = row_send(sent2)
    own2, rs2, *send2 = call(fold(1), info, [mine2, came2, hidden, gains], fold_outs)
    got2 = [col_send(s, k + 1) for k, s in enumerate(send2)]

    def mid(inf, own, rs, hid_ref, gn, og, *refs):
        came, (grad_mid, mix, gain) = refs[:n_col - 1], refs[n_col - 1:]
        total, mean = unfold(own, rs, came)
        full = hid_ref[:rows]
        scale = lax.rsqrt(jnp.sum(full * full, axis=1, keepdims=True) / model + epsilon)
        hid = hid_ref[:rows, :width]
        gm = og[...] + scale * (gn[1:2, :width] * total) - hid * (scale * scale * scale) * (mean / model)
        grad_mid[...] = gm
        mix[...] = gm.astype(bf16)
        gain[...] = jnp.broadcast_to(jnp.sum(total * hid * scale, axis=0, keepdims=True), (8, width))

    grad_mid, gmix0, gain_two = call(
        mid, info, [own2, rs2, hidden, gains, out_grad] + got2,
        [((rows, width), f32), ((rows, width), bf16), ((8, width), f32)],
    )
    gmix = [gmix0] + [col_send(gmix0, k) for k in peers()]
    gmix_o = [row_send(m) for m in gmix]

    acts = [act] + [col_send(act, k) for k in peers()]
    pieces = [piece0] + [col_send(piece0, k) for k in peers()]

    def ffn_grad(inf, ac, pc, gfa, gfb, n2r, out_a, out_b, gf, out):
        gf[:rows] = gfa[...]
        gf[rows:] = gfb[...]
        out[:ff] = dot(ac[...], gf[...], 1, 0).astype(bf16)
        out[ff:] = dot(pc[...], n2r[...], 1, 0).astype(bf16)
        out_a[...] = out[:cut]
        out_b[...] = out[cut:]

    chunks = [chunk_a, chunk_b]
    for k in peers():
        chunk_a, chunk_b = call(
            ffn_grad, info, [acts[k], pieces[k], gf0, gfs_o[0], n2],
            [((cut, width), bf16), ((3 * ff - cut, width), bf16)],
            [pltpu.VMEM((group, width), bf16), pltpu.VMEM((3 * ff, width), bf16)],
        )
        chunks += [chunk_a, chunk_b]

    def mixer_back(inf, sg, taps, m3, *refs):
        go, gx = refs[:n_col], refs[n_col:2 * n_col]
        w = refs[2 * n_col:2 * n_col + n_out]
        wi = refs[2 * n_col + n_out:][:n_col]
        trip_t, mine, sent, tg = refs[3 * n_col + n_out:]
        cc, p = inf[0], inf[2]
        inside = lax.rem(cc * lanes, ho)
        at = pl.ds(pl.multiple_of(inside, lanes), lanes)
        here = (cc * lanes >= ho) == (p == 1)
        gm = jnp.zeros((group, lanes), f32)
        for k in K:
            if k < last_k:
                wk = w[k][pl.ds(pl.multiple_of(cc * lanes, lanes), lanes), :]
            else:
                wk = jnp.where(here, w[k][at, :], w[k + 1][at, :])
            gm = gm + dot(jnp.concatenate([go[k][...], gx[k][...]], axis=0), wk, 1, 1)
        one, two = masks(sg[...], inf[1], rows, group)
        gate_in, gate_out, carried = m3[:, :lanes], m3[:, lanes:2 * lanes], m3[:, 2 * lanes:]
        product = gate_in * carried
        back_one = pltpu.roll(product, 1, 0) * one
        back_two = pltpu.roll(product, 2, 0) * two
        conv = taps[2:3] * product + taps[1:2] * back_one + taps[0:1] * back_two
        gc = gm * gate_out
        gpr = (
            taps[2:3] * gc
            + taps[1:2] * pltpu.roll(gc * one, group - 1, 0)
            + taps[0:1] * pltpu.roll(gc * two, group - 2, 0)
        )
        tg[...] = jnp.zeros((8, lanes), f32)
        tg[0:1] = jnp.sum(gc * back_two, axis=0, keepdims=True)
        tg[1:2] = jnp.sum(gc * back_one, axis=0, keepdims=True)
        tg[2:3] = jnp.sum(gc * product, axis=0, keepdims=True)
        triple = jnp.concatenate([gpr * carried, gm * conv, gpr * gate_in], axis=1)
        trip_t[...] = triple.T.astype(bf16)
        low = triple.astype(bf16)
        for k in K:
            cols = slice(k * width, (k + 1) * width)
            part = dot(low, wi[k][:width], 1, 1)
            mine[:, cols] = part[:rows]
            sent[:, cols] = part[rows:].astype(bf16)

    trip0, mine1, sent1, taps_grad = call(
        mixer_back, info, [seg, conv_taps, mix3] + gmix + gmix_o + outs_r + w_in,
        [((3 * lanes, group), bf16), ((rows, model), f32), ((rows, model), bf16), ((8, lanes), f32)],
    )
    trips = [trip0] + [col_send(trip0, k) for k in peers()]

    def mix_grad(inf, n1r, ga, gb, *refs):
        count = len(refs[:-1]) // 3
        gm = refs[-1]
        gm[:rows] = ga[...]
        gm[rows:] = gb[...]
        for tr, mx, out in zip(refs[:count], refs[count:2 * count], refs[2 * count:-1]):
            out[:3 * lanes] = dot(tr[...], n1r[...], 1, 0).astype(bf16)
            out[3 * lanes:] = dot(mx[...].T, gm[...], 1, 0).astype(bf16)

    for part in (slice(0, 1), slice(1, n_col)):
        chunks += call(
            mix_grad, info, [n1, gmix[0], gmix_o[0]] + trips[part] + mixeds[part],
            [((4 * lanes, width), bf16)] * len(trips[part]), [pltpu.VMEM((group, width), bf16)],
        )

    came1 = row_send(sent1)
    own1, rs1, *send1 = call(fold(0), info, [mine1, came1, tok, gains], fold_outs)
    got1 = [col_send(s, k + 1) for k, s in enumerate(send1)]

    def last(inf, own, rs, tk, gn, gmid, gtwo, *refs):
        came, (out, gain) = refs[:n_col - 1], refs[n_col - 1:]
        total, mean = unfold(own, rs, came)
        full = tk[:rows]
        scale = lax.rsqrt(jnp.sum(full * full, axis=1, keepdims=True) / model + epsilon)
        part = tk[:rows, :width]
        out[...] = gmid[...] + scale * (gn[0:1, :width] * total) - part * (scale * scale * scale) * (mean / model)
        gain[...] = gtwo[...]
        gain[0:1] = jnp.sum(total * part * scale, axis=0, keepdims=True)

    in_grad, gain_pair = call(
        last, info, [own1, rs1, tok, gains, grad_mid, gain_two] + got1,
        [((rows, width), f32), ((8, width), f32)],
    )

    gain_came = row_send(gain_pair)

    def ffn_out(inf, dw, hid, ga, gb, tg, *refs):
        pcs, (mine, sent, small) = refs[:n_col], refs[n_col:]
        acc = jnp.zeros((group, width), f32)
        for k in K:
            at = pl.ds(pl.multiple_of((inf[0] ^ k) * ff, 32), ff)
            acc = acc + dot(pcs[k][...].T, dw[at, :], 1, 0)
        mine[...] = acc[:rows] + hid[:rows, :width]
        sent[...] = acc[rows:]
        wide = jnp.concatenate([tg[...], jnp.zeros((8, width - lanes), f32)], axis=1) if width > lanes else tg[...]
        small[...] = jnp.concatenate([ga[...] + gb[...], wide], axis=0).astype(bf16)

    out_mine, out_sent, small = call(
        ffn_out, info, [down_weight, hidden, gain_pair, gain_came, taps_grad] + acts,
        [((rows, width), f32)] * 2 + [((16, width), bf16)],
    )
    out_came = row_send(out_sent)

    chunks.append(small)
    sums = dp_sums(chunks)

    def place_down(inf, *refs):
        parts, (oa, ob, down, out) = refs[:2 * n_col], refs[2 * n_col:]
        out[...] = oa[...] + ob[...]
        for k in K:
            at = pl.ds(pl.multiple_of((inf[0] ^ k) * ff, 32), ff)
            down[at, :] = jnp.where(inf[3] == 1, parts[2 * k + 1][:ff], parts[2 * k][:ff]).astype(f32)

    down_sum, block_out = call(
        place_down, info, [x for s in sums[:2 * n_col:2] for x in s] + [out_mine, out_came],
        [((hidden_ff, width), f32), ((rows, width), f32)],
    )

    def ffn_place(inf, *refs):
        parts, (gate, up, gt, ut) = refs[:4 * n_col], refs[4 * n_col:]
        far = inf[3] == 1
        for k in K:
            ha, ca, hb, cb = parts[4 * k:4 * k + 4]
            at = (inf[0] ^ k) * ff
            near = cut - ff
            gt[pl.ds(pl.multiple_of(at, 32), near), :] = jnp.where(far, ca[ff:cut], ha[ff:cut])
            gt[pl.ds(pl.multiple_of(at + near, 32), ff - near), :] = jnp.where(far, cb[:ff - near], hb[:ff - near])
            ut[pl.ds(pl.multiple_of(at, 32), ff), :] = jnp.where(far, cb[ff - near:cut], hb[ff - near:cut])
        gate[...] = gt[...].T.astype(f32)
        up[...] = ut[...].T.astype(f32)

    gate_sum, up_sum = call(
        ffn_place, info, [x for s in sums[:2 * n_col] for x in s],
        [((width, hidden_ff), f32)] * 2, [pltpu.VMEM((hidden_ff, width), bf16)] * 2,
    )

    def mix_place(inf, *refs):
        held_refs, came_refs = refs[:n_col], refs[n_col + 1:2 * n_col + 1]
        win, wout, g1, g2, tg = refs[2 * n_col + 2:]
        far = inf[3] == 1
        small = jnp.where(far, refs[2 * n_col + 1][...], refs[n_col][...]).astype(f32)
        g1[...] = small[0:1]
        g2[...] = small[1:2]
        tg[...] = small[8:11, :lanes]
        for k in K:
            at = pl.ds(pl.multiple_of((inf[0] ^ k) * lanes, lanes), lanes)
            for t in range(4):
                rr = slice(t * lanes, (t + 1) * lanes)
                got = jnp.where(far, came_refs[k][rr], held_refs[k][rr])
                if t < 3:
                    win[t, :, at] = got.T.astype(f32)
                else:
                    wout[at, :] = got.astype(f32)

    in_sum, out_sum, small_one, small_two, small_taps = call(
        mix_place, info, [s[0] for s in sums[2 * n_col:]] + [s[1] for s in sums[2 * n_col:]],
        [((3, width, span), f32), ((span, width), f32)] + [((1, width), f32)] * 2 + [((3, lanes), f32)],
    )
    return (
        block_out,
        in_grad,
        small_one.reshape(width),
        jnp.transpose(in_sum, (1, 0, 2)),
        small_taps,
        out_sum,
        small_two.reshape(width),
        gate_sum,
        up_sum,
        down_sum,
    )


def solution(mesh):
    token = P(("dp", "row"), "col")
    feature, tap = P("col"), P(None, ("row", "col"))
    split_in, split_up, split_down = P("col", None, "row"), P("col", "row"), P("row", "col")
    weights = (feature, split_in, tap, split_down, feature, split_up, split_up, split_down)
    in_specs = (token, P("dp"), *weights, token)
    out_specs = (token, token, *weights)

    return jax.shard_map(per_device, mesh=mesh, in_specs=in_specs, out_specs=out_specs, check_vma=False)
```
